256 devices in a mesh: dp: 32 (over y, x, core), mp: 8 (over z).
Axes of the slice: x: 4, y: 4, z: 8, core: 2. Of those that a mesh axis runs over, the one named last changes fastest.
Arguments:
- saved_query: bfloat16 [32768, 4096], P('dp', 'mp'), may hold values from -80 to 80
- saved_key: bfloat16 [32768, 1024], P('dp', 'mp'), may hold values from -16 to 16
- saved_value: bfloat16 [32768, 1024], P('dp', 'mp'), may hold values from -6 to 6
- grad_output: bfloat16 [32768, 4096], P('dp', 'mp'), may hold values from -24 to 24
- unit_server: int32 [1024], P('dp'), may hold values from 0 to 31, as said below
- unit_place: int32 [1024], P('dp'), may hold values from 0 to 31, as said below
- doc_length: int32 [128], P('dp'), may hold values from 1 to 256
- query_weight: bfloat16 [4096, 4096], P(None, 'mp'), may hold values from -0.078125 to 0.078125
- key_weight: bfloat16 [4096, 1024], P(None, 'mp'), may hold values from -0.078125 to 0.078125
- value_weight: bfloat16 [4096, 1024], P(None, 'mp'), may hold values from -0.078125 to 0.078125
Outputs:
- grad_input: float32 [32768, 4096], P('dp', 'mp')
The draws below stay inside these ranges and needn't reach their ends.
Inputs may be any that keep to these rules, and one draw needn't show every extreme that they name: `unit_server`: each server receives exactly 32 units, exactly one from the units of each device along dp; the units of one document block come from 8 different devices. The pairs (unit_server, unit_place) are all different, so each server's places 0 to 31 are each taken once.
All inputs are finite; a program needn't handle non-finite values.
Results may differ from the reference program's by a relative error of at most 0.011.
Values may be sent and summed in bfloat16 or wider, within the bound.
A program may use at most 128 MiB of HBM per device.

```python
import math
import jax
import jax.numpy as jnp
from jax import lax

D = 4096
QHEADS = 32
KVHEADS = 8
HEAD = 128
UNIT = 32
DOC_UNITS = 8
U_DEV = 32
DOCS = 128
TOKENS = 32768
N_DP = 32


def draw_pair(key):
    base = jax.random.fold_in(key, 31)
    query_key, key_key = jax.random.split(base, 2)
    keys = jax.random.normal(key_key, (TOKENS, KVHEADS * HEAD), jnp.float32)
    queries = jax.random.normal(query_key, (TOKENS, QHEADS * HEAD), jnp.float32)
    return (queries, keys)


def draw_saved_query(key, part):
    return draw_pair(key)[0].astype(jnp.bfloat16)


def draw_saved_key(key, part):
    return draw_pair(key)[1].astype(jnp.bfloat16)


def draw_routing(key):
    base = jax.random.fold_in(key, 57)
    first, second, third, fourth, fifth = jax.random.split(base, 5)
    server_count = TOKENS // (UNIT * U_DEV)
    server_order = jax.random.permutation(first, server_count)
    trunk_order = jax.random.permutation(second, server_count)
    offsets = jax.random.permutation(third, server_count)[:U_DEV]
    ranks = jax.random.randint(fourth, (server_count, U_DEV), 0, 1 << 20) * U_DEV + jnp.arange(U_DEV)[None, :]
    slot_of = jnp.argsort(ranks, axis=1)
    servers = server_order[(trunk_order[:, None] + offsets[slot_of]) % server_count]
    place_ranks = jax.random.randint(fifth, (server_count, U_DEV), 0, 1 << 20) * U_DEV + jnp.arange(U_DEV)[None, :]
    place_table = jnp.argsort(place_ranks, axis=1)
    places = place_table[servers, slot_of]
    return (servers.reshape(-1).astype(jnp.int32), places.reshape(-1).astype(jnp.int32))


def draw_unit_server(key, part):
    return draw_routing(key)[0]


def draw_unit_place(key, part):
    return draw_routing(key)[1]


def plant(values, key, smallest, top_value):
    spot = [jax.random.randint(jax.random.fold_in(key, axis), (), 0, length) for axis, length in enumerate(values.shape)]
    longest = values.shape.index(max(values.shape))
    neighbour = spot[:longest] + [(spot[longest] + 1) % values.shape[longest]] + spot[longest + 1:]
    return values.at[tuple(spot)].set(smallest).at[tuple(neighbour)].set(top_value)


def block_levels(stream_key, dims, cuts, smallest, top_value):
    def one(axis_at, shards_of):
        draws = jax.random.uniform(jax.random.fold_in(jax.random.fold_in(stream_key, 6), axis_at), (shards_of,), jnp.float32, smallest / len(cuts), top_value / len(cuts))
        return jnp.repeat(jnp.exp(draws), dims[axis_at] // shards_of).reshape((-1,) + (1,) * (len(dims) - axis_at - 1))

    factor_of = one(*cuts[0])
    for cut in cuts[1:]:
        factor_of = factor_of * one(*cut)
    return factor_of


def scatter_about(own_key, shape, deviation, most, cuts=(), kind=jnp.bfloat16):
    array = deviation * jax.random.normal(own_key, shape, jnp.float32)
    if cuts:
        array = array * block_levels(own_key, shape, cuts, -0.22, 0.18)
    return jnp.clip(array, -most, most).astype(kind)


def setup_inputs(seed: int = 0) -> dict:
    key_list = jax.random.split(jax.random.key(seed), 11)
    saved_query = draw_saved_query(jax.random.fold_in(key_list[10], 71), 0)
    saved_key = draw_saved_key(jax.random.fold_in(key_list[10], 71), 0)
    saved_value = scatter_about(key_list[2], (TOKENS, KVHEADS * HEAD), 1.0, 6.0, ((0, 32), (1, 8)))
    grad_output = scatter_about(key_list[3], (TOKENS, QHEADS * HEAD), 4.0, 24.0, ((0, 32), (1, 8)))
    unit_server = draw_unit_server(jax.random.fold_in(key_list[10], 71), 0)
    unit_place = draw_unit_place(jax.random.fold_in(key_list[10], 71), 0)
    doc_length = plant(jax.random.randint(key_list[6], (DOCS,), 1, DOC_UNITS * UNIT + 1), jax.random.fold_in(key_list[6], 1), 1, DOC_UNITS * UNIT).astype(jnp.int32)
    query_weight = scatter_about(key_list[7], (D, QHEADS * HEAD), ((QHEADS + 2 * KVHEADS) * HEAD) ** -0.5, 0.078125, ((1, 8),))
    key_weight = scatter_about(key_list[8], (D, KVHEADS * HEAD), ((QHEADS + 2 * KVHEADS) * HEAD) ** -0.5, 0.078125, ((1, 8),))
    value_weight = scatter_about(key_list[9], (D, KVHEADS * HEAD), ((QHEADS + 2 * KVHEADS) * HEAD) ** -0.5, 0.078125, ((1, 8),))
    return {"saved_query": saved_query, "saved_key": saved_key, "saved_value": saved_value, "grad_output": grad_output, "unit_server": unit_server, "unit_place": unit_place, "doc_length": doc_length, "query_weight": query_weight, "key_weight": key_weight, "value_weight": value_weight}


def doc_backward(doc_query, doc_key, doc_value, doc_grad, length):
    block_rows = doc_query.shape[0]
    group_size = QHEADS // KVHEADS
    score_scale = 1.0 / math.sqrt(HEAD)
    highest = lax.Precision.HIGHEST
    rows_index = jnp.arange(block_rows, dtype=jnp.int32)
    live_rows = (rows_index < length).astype(doc_grad.dtype)
    masked = (doc_grad * live_rows[:, None]).astype(jnp.float32).reshape(block_rows, KVHEADS, group_size, HEAD)
    queries = doc_query.astype(jnp.float32).reshape(block_rows, KVHEADS, group_size, HEAD)
    keys = doc_key.astype(jnp.float32).reshape(block_rows, KVHEADS, HEAD)
    values = doc_value.astype(jnp.float32).reshape(block_rows, KVHEADS, HEAD)
    allowed = (rows_index[None, :] <= rows_index[:, None]) & (rows_index[None, :] < length)
    scores = jnp.einsum('ikgd,jkd->kgij', queries, keys, precision=highest) * score_scale
    scores = jnp.where(allowed, scores, -1e+30)
    row_peak = lax.optimization_barrier(jnp.max(scores, axis=-1, keepdims=True))
    expanded = jnp.where(allowed, jnp.exp(scores - row_peak), 0.0)
    attention = expanded / lax.optimization_barrier(jnp.sum(expanded, axis=-1, keepdims=True))
    attention_low = lax.optimization_barrier(attention.astype(jnp.bfloat16)).astype(jnp.float32)
    attended = jnp.einsum('kgij,jkd->ikgd', attention_low, values, precision=highest)
    row_delta = lax.optimization_barrier(jnp.sum(masked * attended, axis=-1))
    prob_grad = jnp.einsum('ikgd,jkd->kgij', masked, values, precision=highest)
    score_grad = attention * (prob_grad - jnp.transpose(row_delta, (1, 2, 0))[..., None])
    score_low = lax.optimization_barrier(score_grad.astype(jnp.bfloat16)).astype(jnp.float32)
    query_grad = jnp.einsum('kgij,jkd->ikgd', score_low, keys, precision=highest) * score_scale
    key_grad = jnp.einsum('kgij,ikgd->jkd', score_low, queries, precision=highest) * score_scale
    value_grad = jnp.einsum('kgij,ikgd->jkd', attention_low, masked, precision=highest)
    return (query_grad.reshape(block_rows, QHEADS * HEAD).astype(jnp.bfloat16), key_grad.reshape(block_rows, KVHEADS * HEAD).astype(jnp.bfloat16), value_grad.reshape(block_rows, KVHEADS * HEAD).astype(jnp.bfloat16))

def reference(saved_query, saved_key, saved_value, grad_output, unit_server, unit_place, doc_length, query_weight, key_weight, value_weight):
    unit_count = N_DP * U_DEV
    block_rows = DOC_UNITS * UNIT
    target = (unit_server * U_DEV + unit_place).astype(jnp.int32)

    def to_docs(tensor):
        columns = tensor.shape[1]
        pieces = tensor.reshape(unit_count, UNIT, columns)
        ordered = jnp.zeros_like(pieces).at[target].set(pieces)
        return ordered.reshape(unit_count // DOC_UNITS, block_rows, columns)

    def one_doc(element):
        return doc_backward(element[0], element[1], element[2], element[3], element[4])
    grads = lax.map(one_doc, (to_docs(saved_query), to_docs(saved_key), to_docs(saved_value), to_docs(grad_output), doc_length.astype(jnp.int32)))

    def to_tokens(tensor):
        columns = tensor.shape[2]
        pieces = tensor.reshape(unit_count, UNIT, columns)
        return pieces[target].reshape(unit_count * UNIT, columns)
    numbers = (((1,), (1,)), ((), ()))
    summed = lax.dot_general(to_tokens(grads[0]), query_weight, numbers, preferred_element_type=jnp.float32)
    summed = summed + lax.dot_general(to_tokens(grads[1]), key_weight, numbers, preferred_element_type=jnp.float32)
    summed = summed + lax.dot_general(to_tokens(grads[2]), value_weight, numbers, preferred_element_type=jnp.float32)
    return summed
```

```python
import functools
import math

import jax
import jax.numpy as jnp
from jax import lax
from jax.experimental import pallas as pl
from jax.experimental.pallas import tpu as pltpu
from jax.sharding import PartitionSpec as P

HEAD = 128
DOC_UNITS = 8
MESH = pl.DeviceIdType.MESH
NT = (((1,), (1,)), ((), ()))
NN = (((1,), (0,)), ((), ()))
TN = (((0,), (0,)), ((), ()))
CHUNK_UNITS = 4
GRID_Y, GRID_X, CORES = 4, 4, 2


def dot(a, b, numbers):
    return lax.dot_general(a, b, numbers, preferred_element_type=jnp.float32)


def kernel(
    n_dp,
    n_mp,
    server_ref,
    place_ref,
    length_ref,
    q_hbm,
    k_hbm,
    v_hbm,
    g_hbm,
    wq_hbm,
    wk_hbm,
    wv_hbm,
    out_hbm,
    in_buf,
    stage,
    recv,
    table_out,
    table_in,
    inv_vec,
    inv_smem,
    where_vec,
    where_smem,
    weights,
    grads,
    lhs,
    ring_send,
    ring_recv,
    out_buf,
    in_sem,
    weight_sem,
    small_sem,
    a2a_send,
    a2a_recv,
    table_send,
    table_recv,
    ring_send_sem,
    ring_recv_sem,
    back_send,
    back_recv,
):
    me = lax.axis_index("dp")
    z = lax.axis_index("mp")
    units, unit_rows, q_cols = q_hbm.shape
    kv_cols = k_hbm.shape[2]
    heads = q_cols // HEAD
    docs = units // DOC_UNITS
    g_at, k_at, v_at = q_cols, 2 * q_cols, 2 * q_cols + kv_cols
    core = lax.rem(me, CORES)
    x = lax.rem(me // CORES, GRID_X)
    y = me // (CORES * GRID_X)

    def peer(offset):
        dc = lax.rem(offset, CORES)
        dx = lax.rem(offset // CORES, GRID_X)
        dy = offset // (CORES * GRID_X)
        return (
            lax.rem(y + dy, GRID_Y) * GRID_X + lax.rem(x + dx, GRID_X)
        ) * CORES + lax.rem(core + dc, CORES)

    loads = [
        pltpu.make_async_copy(q_hbm, in_buf.at[:, :, pl.ds(0, q_cols)], in_sem.at[0]),
        pltpu.make_async_copy(g_hbm, in_buf.at[:, :, pl.ds(g_at, q_cols)], in_sem.at[1]),
        pltpu.make_async_copy(k_hbm, in_buf.at[:, :, pl.ds(k_at, kv_cols)], in_sem.at[2]),
        pltpu.make_async_copy(v_hbm, in_buf.at[:, :, pl.ds(v_at, kv_cols)], in_sem.at[3]),
    ]
    for copy in loads:
        copy.start()
    weight_loads = [
        pltpu.make_async_copy(wq_hbm, weights.at[:, pl.ds(0, q_cols)], weight_sem.at[0]),
        pltpu.make_async_copy(wk_hbm, weights.at[:, pl.ds(q_cols, kv_cols)], weight_sem.at[1]),
        pltpu.make_async_copy(
            wv_hbm, weights.at[:, pl.ds(q_cols + kv_cols, kv_cols)], weight_sem.at[2]
        ),
    ]

    barrier = pltpu.get_barrier_semaphore()

    def greet(o, carry):
        pl.semaphore_signal(barrier, inc=1, device_id={"dp": peer(o)}, device_id_type=MESH)
        return carry

    lax.fori_loop(1, n_dp, greet, 0)
    right, left = lax.rem(z + 1, n_mp), lax.rem(z + n_mp - 1, n_mp)
    for near in (left, right):
        pl.semaphore_signal(barrier, inc=1, device_id={"mp": near}, device_id_type=MESH)

    lanes = lax.broadcasted_iota(jnp.int32, (8, 128), 1)
    unit_of = jnp.zeros((8, 128), jnp.int32)
    place_of = jnp.zeros((8, 128), jnp.int32)
    for u in range(units):
        hit = lanes == server_ref[u]
        unit_of = jnp.where(hit, u, unit_of)
        place_of = jnp.where(hit, place_ref[u], place_of)
    inv_vec[...] = unit_of
    table_out[...] = place_of
    table_in[me] = place_of
    to_smem = pltpu.make_async_copy(inv_vec, inv_smem, small_sem.at[0])
    to_smem.start()
    to_smem.wait()
    for copy in loads:
        copy.wait()

    pl.semaphore_wait(barrier, n_dp - 1 + 2)

    def table_copy(o):
        to = peer(o)
        return pltpu.make_async_remote_copy(
            src_ref=table_out,
            dst_ref=table_in.at[me],
            send_sem=table_send.at[to],
            recv_sem=table_recv.at[me],
            device_id={"dp": to},
            device_id_type=MESH,
        )

    def unit_copy(o):
        to = peer(o)
        return pltpu.make_async_remote_copy(
            src_ref=stage.at[to],
            dst_ref=recv.at[me],
            send_sem=a2a_send.at[to],
            recv_sem=a2a_recv.at[me],
            device_id={"dp": to},
            device_id_type=MESH,
        )

    def send_unit(o, carry):
        table_copy(o).start()
        to = peer(o)
        stage[to] = in_buf[inv_smem[0, to]]
        unit_copy(o).start()
        return carry

    lax.fori_loop(1, n_dp, send_unit, 0)
    recv[me] = in_buf[inv_smem[0, me]]
    for copy in weight_loads:
        copy.start()

    def table_arrived(o, carry):
        frm = peer(o)
        pltpu.make_async_remote_copy(
            src_ref=table_out,
            dst_ref=table_in.at[frm],
            send_sem=table_send.at[frm],
            recv_sem=table_recv.at[frm],
            device_id={"dp": frm},
            device_id_type=MESH,
        ).wait()
        return carry

    lax.fori_loop(1, n_dp, table_arrived, 0)
    table = table_in[:, 0, :]
    wide = lax.broadcasted_iota(jnp.int32, (units, 128), 1)
    tall = lax.broadcasted_iota(jnp.int32, (units, 128), 0)
    place_col = jnp.sum(jnp.where(wide == me, table, 0), axis=1, keepdims=True)
    source = jnp.max(jnp.where(place_col == wide, tall, 0), axis=0, keepdims=True)
    where_vec[pl.ds(0, units), :] = jnp.broadcast_to(place_col, (units, 128))
    where_vec[pl.ds(units, 8), :] = jnp.broadcast_to(source, (8, 128))
    to_smem = pltpu.make_async_copy(where_vec, where_smem, small_sem.at[1])
    to_smem.start()
    to_smem.wait()

    def unit_arrived(o, carry):
        frm = peer(o)
        pltpu.make_async_remote_copy(
            src_ref=stage.at[frm],
            dst_ref=recv.at[frm],
            send_sem=a2a_send.at[frm],
            recv_sem=a2a_recv.at[frm],
            device_id={"dp": frm},
            device_id_type=MESH,
        ).wait()
        return carry

    lax.fori_loop(1, n_dp, unit_arrived, 0)

    block = DOC_UNITS * unit_rows
    score_scale = 1.0 / math.sqrt(HEAD)
    exponent_scale = score_scale * math.log2(math.e)

    def one_doc(doc, carry):
        length = length_ref[doc]
        sources = [where_smem[units, doc * DOC_UNITS + i] for i in range(DOC_UNITS)]

        def rows(at):
            return jnp.concatenate(
                [recv[s, :, pl.ds(at, HEAD)] for s in sources], axis=0
            )

        key_at = lax.broadcasted_iota(jnp.int32, (block, block), 0)
        query_at = lax.broadcasted_iota(jnp.int32, (block, block), 1)
        allowed = (key_at <= query_at) & (key_at < length)
        live = lax.broadcasted_iota(jnp.int32, (block, HEAD), 0) < length
        keys, values = rows(k_at), rows(v_at)
        key_grad = jnp.zeros((block, HEAD), jnp.float32)
        value_grad = jnp.zeros((block, HEAD), jnp.float32)

        def store(at, value):
            low = value.astype(jnp.bfloat16)
            for i in range(DOC_UNITS):
                grads[doc * DOC_UNITS + i, :, pl.ds(at, HEAD)] = low[
                    i * unit_rows : (i + 1) * unit_rows
                ]

        for head in range(heads):
            queries = rows(head * HEAD)
            masked = rows(g_at + head * HEAD)
            masked = jnp.where(live, masked, jnp.zeros_like(masked))
            scores = jnp.where(allowed, dot(keys, queries, NT), -1e30)
            peak = jnp.max(scores, axis=0, keepdims=True)
            expanded = jnp.exp2((scores - peak) * exponent_scale)
            probs = expanded * (1.0 / jnp.sum(expanded, axis=0, keepdims=True))
            probs_low = probs.astype(jnp.bfloat16)
            prob_grad = dot(values, masked, NT)
            delta = jnp.sum(probs_low.astype(jnp.float32) * prob_grad, axis=0, keepdims=True)
            score_low = (probs * (prob_grad - delta)).astype(jnp.bfloat16)
            value_grad += dot(probs_low, masked, NN)
            key_grad += dot(score_low, queries, NN)
            store(head * HEAD, dot(score_low, keys, TN) * score_scale)
        store(q_cols, key_grad * score_scale)
        store(q_cols + kv_cols, value_grad)
        return carry

    lax.fori_loop(0, docs, one_doc, 0)
    for copy in weight_loads:
        copy.wait()

    chunks = units // CHUNK_UNITS
    chunk_rows = CHUNK_UNITS * unit_rows
    half = chunk_rows // 2
    out_cols = out_hbm.shape[2]
    far = n_mp // 2

    def part(chunk, distance, first, count):
        column = lax.rem(z + distance, n_mp) * out_cols
        return dot(
            lhs[chunk, pl.ds(first, count), :],
            weights[pl.ds(pl.multiple_of(column, out_cols), out_cols), :],
            NT,
        )

    def ring_copy(chunk, way, step):
        first, count = (0, chunk_rows) if step else (way * half, half)
        return pltpu.make_async_remote_copy(
            src_ref=ring_send.at[chunk, way, step, pl.ds(first, count), :],
            dst_ref=ring_recv.at[chunk, way, step, pl.ds(first, count), :],
            send_sem=ring_send_sem.at[chunk, way, step],
            recv_sem=ring_recv_sem.at[chunk, way, step],
            device_id={"mp": left if way else right},
            device_id_type=MESH,
        )

    def back_copy(chunk, i):
        to = peer(chunk * CHUNK_UNITS + i)
        return pltpu.make_async_remote_copy(
            src_ref=out_buf.at[chunk * CHUNK_UNITS + i],
            dst_ref=out_hbm.at[me],
            send_sem=back_send.at[to],
            recv_sem=back_recv.at[me],
            device_id={"dp": to},
            device_id_type=MESH,
        )

    own_copy = pltpu.make_async_copy(out_buf.at[0], out_hbm.at[me], small_sem.at[2])

    def slot(t, carry):
        @pl.when(t < chunks)
        def _():
            for i in range(CHUNK_UNITS):
                s = peer(t * CHUNK_UNITS + i)
                lhs[t, pl.ds(i * unit_rows, unit_rows), :] = grads[where_smem[s, 0]]

        for step in range(far):
            chunk = t - step

            @pl.when((chunk >= 0) & (chunk < chunks))
            def _(chunk=chunk, step=step):
                for way in range(2):
                    distance = n_mp - far + step if way else far - step
                    if step == 0:
                        first, count = way * half, half
                        ring_send[chunk, way, step, pl.ds(first, count), :] = part(
                            chunk, distance, first, count
                        ).astype(jnp.bfloat16)
                    else:
                        ring_copy(chunk, way, step - 1).wait_recv()
                        for p in range(2):
                            first, count = p * half, half
                            total = part(chunk, distance, first, count)
                            if step > 1 or p == way:
                                total += ring_recv[
                                    chunk, way, step - 1, pl.ds(first, count), :
                                ].astype(jnp.float32)
                            ring_send[chunk, way, step, pl.ds(first, count), :] = total.astype(
                                jnp.bfloat16
                            )
                    ring_copy(chunk, way, step).start()

        chunk = t - far

        @pl.when(chunk >= 0)
        def _():
            for way in range(2):
                ring_copy(chunk, way, far - 1).wait_recv()
            for i in range(CHUNK_UNITS):
                first = i * unit_rows
                total = part(chunk, 0, first, unit_rows)
                for way in range(2):
                    total += ring_recv[
                        chunk, way, far - 1, pl.ds(first, unit_rows), :
                    ].astype(jnp.float32)
                out_buf[chunk * CHUNK_UNITS + i] = total.astype(jnp.bfloat16)
                if i == 0:

                    @pl.when(chunk == 0)
                    def _():
                        own_copy.start()

                    @pl.when(chunk > 0)
                    def _():
                        back_copy(chunk, 0).start()
                else:
                    back_copy(chunk, i).start()

        return carry

    lax.fori_loop(0, chunks + far, slot, 0)
    own_copy.wait()

    def ring_done(chunk, carry):
        for way in range(2):
            for step in range(far):
                ring_copy(chunk, way, step).wait_send()
        return carry

    lax.fori_loop(0, chunks, ring_done, 0)

    def back_arrived(o, carry):
        frm = peer(o)
        pltpu.make_async_remote_copy(
            src_ref=out_buf.at[o],
            dst_ref=out_hbm.at[frm],
            send_sem=back_send.at[frm],
            recv_sem=back_recv.at[frm],
            device_id={"dp": frm},
            device_id_type=MESH,
        ).wait()
        return carry

    lax.fori_loop(1, n_dp, back_arrived, 0)


def local(
    saved_query,
    saved_key,
    saved_value,
    grad_output,
    unit_server,
    unit_place,
    doc_length,
    query_weight,
    key_weight,
    value_weight,
):
    n_dp, n_mp = lax.axis_size("dp"), lax.axis_size("mp")
    units = unit_server.shape[0]
    unit_rows = saved_query.shape[0] // units
    q_cols, kv_cols = saved_query.shape[1], saved_key.shape[1]
    out_all = query_weight.shape[0]
    out_cols = out_all // n_mp
    k_cols = q_cols + 2 * kv_cols
    in_cols = 2 * q_cols + 2 * kv_cols
    chunks = units // CHUNK_UNITS
    chunk_rows = CHUNK_UNITS * unit_rows
    far = n_mp // 2
    low = jnp.bfloat16

    def split(a):
        return a.reshape(units, unit_rows, a.shape[1])

    smem = pl.BlockSpec(memory_space=pltpu.SMEM)
    hbm = pl.BlockSpec(memory_space=pl.ANY)
    dma = pltpu.SemaphoreType.DMA
    back = pl.pallas_call(
        functools.partial(kernel, n_dp, n_mp),
        out_shape=jax.ShapeDtypeStruct((n_dp, unit_rows, out_cols), low),
        in_specs=[smem] * 3 + [hbm] * 7,
        out_specs=hbm,
        scratch_shapes=[
            pltpu.VMEM((units, unit_rows, in_cols), low),
            pltpu.VMEM((n_dp, unit_rows, in_cols), low),
            pltpu.VMEM((n_dp, unit_rows, in_cols), low),
            pltpu.VMEM((8, 128), jnp.int32),
            pltpu.VMEM((n_dp, 8, 128), jnp.int32),
            pltpu.VMEM((8, 128), jnp.int32),
            pltpu.SMEM((8, 128), jnp.int32),
            pltpu.VMEM((units + 8, 128), jnp.int32),
            pltpu.SMEM((units + 8, 128), jnp.int32),
            pltpu.VMEM((out_all, k_cols), low),
            pltpu.VMEM((units, unit_rows, k_cols), low),
            pltpu.VMEM((chunks, chunk_rows, k_cols), low),
            pltpu.VMEM((chunks, 2, far, chunk_rows, out_cols), low),
            pltpu.VMEM((chunks, 2, far, chunk_rows, out_cols), low),
            pltpu.VMEM((units, unit_rows, out_cols), low),
            dma((4,)),
            dma((3,)),
            dma((3,)),
            dma((n_dp,)),
            dma((n_dp,)),
            dma((n_dp,)),
            dma((n_dp,)),
            dma((chunks, 2, far)),
            dma((chunks, 2, far)),
            dma((n_dp,)),
            dma((n_dp,)),
        ],
        compiler_params=pltpu.CompilerParams(
            collective_id=0, has_side_effects=True, vmem_limit_bytes=60 * 1024 * 1024
        ),
        name="attention_backward_exchange",
    )(
        unit_server,
        unit_place,
        doc_length,
        split(saved_query),
        split(saved_key),
        split(saved_value),
        split(grad_output),
        query_weight,
        key_weight,
        value_weight,
    )
    return back[unit_server].astype(jnp.float32).reshape(units * unit_rows, out_cols)


def solution(mesh):
    placed = (
        P("dp", "mp"),
        P("dp", "mp"),
        P("dp", "mp"),
        P("dp", "mp"),
        P("dp"),
        P("dp"),
        P("dp"),
        P(None, "mp"),
        P(None, "mp"),
        P(None, "mp"),
    )
    return jax.shard_map(
        local, mesh=mesh, in_specs=placed, out_specs=P("dp", "mp"), check_vma=False
    )
```

```python
import functools
import math

import jax
import jax.numpy as jnp
from jax import lax
from jax.experimental import pallas as pl
from jax.experimental.pallas import tpu as pltpu
from jax.sharding import PartitionSpec as P

HEAD = 128
DOC_UNITS = 8
MESH = pl.DeviceIdType.MESH
NT = (((1,), (1,)), ((), ()))
NN = (((1,), (0,)), ((), ()))
TN = (((0,), (0,)), ((), ()))
CHUNK_UNITS = 4
SETTLE_STEPS = 4
GRID_Y, GRID_X, CORES = 4, 4, 2


def dot(a, b, numbers):
    return lax.dot_general(a, b, numbers, preferred_element_type=jnp.float32)


def kernel(
    n_dp,
    n_mp,
    phases,
    server_ref,
    place_ref,
    length_ref,
    q_hbm,
    k_hbm,
    v_hbm,
    g_hbm,
    wq_hbm,
    wk_hbm,
    wv_hbm,
    out_hbm,
    *scratch,
):
    count = len(phases)
    held, stage, recv = scratch[:count], scratch[count : 2 * count], scratch[2 * count : 3 * count]
    (
        table_out,
        table_in,
        inv_vec,
        inv_smem,
        where_vec,
        where_smem,
        weights,
        kv_total,
        grads,
        lhs,
        ring_send,
        ring_recv,
        out_buf,
        in_sem,
        weight_sem,
        small_sem,
        a2a_send,
        a2a_recv,
        table_send,
        table_recv,
        ring_send_sem,
        ring_recv_sem,
        back_send,
        back_recv,
    ) = scratch[3 * count :]
    me = lax.axis_index("dp")
    z = lax.axis_index("mp")
    units, unit_rows, q_cols = q_hbm.shape
    kv_cols = k_hbm.shape[2]
    docs = units // DOC_UNITS
    core = lax.rem(me, CORES)
    x = lax.rem(me // CORES, GRID_X)
    y = me // (CORES * GRID_X)

    def peer(offset):
        dc = lax.rem(offset, CORES)
        dx = lax.rem(offset // CORES, GRID_X)
        dy = offset // (CORES * GRID_X)
        return (
            lax.rem(y + dy, GRID_Y) * GRID_X + lax.rem(x + dx, GRID_X)
        ) * CORES + lax.rem(core + dc, CORES)

    loads = []
    for p, heads in enumerate(phases):
        pieces = [] if p else [(k_hbm, 0, kv_cols), (v_hbm, 0, kv_cols)]
        for head in heads:
            pieces += [(q_hbm, head * HEAD, HEAD), (g_hbm, head * HEAD, HEAD)]
        at = 0
        for n, (ref, first, width) in enumerate(pieces):
            loads.append(
                (
                    p,
                    pltpu.make_async_copy(
                        ref.at[:, :, pl.ds(first, width)],
                        held[p].at[:, :, pl.ds(at, width)],
                        in_sem.at[len(loads)],
                    ),
                )
            )
            at += width
    for _, copy in loads:
        copy.start()
    weight_loads = [
        pltpu.make_async_copy(wq_hbm, weights.at[:, pl.ds(0, q_cols)], weight_sem.at[0]),
        pltpu.make_async_copy(wk_hbm, weights.at[:, pl.ds(q_cols, kv_cols)], weight_sem.at[1]),
        pltpu.make_async_copy(
            wv_hbm, weights.at[:, pl.ds(q_cols + kv_cols, kv_cols)], weight_sem.at[2]
        ),
    ]

    barrier = pltpu.get_barrier_semaphore()

    def greet(o, carry):
        pl.semaphore_signal(barrier, inc=1, device_id={"dp": peer(o)}, device_id_type=MESH)
        return carry

    lax.fori_loop(1, n_dp, greet, 0)
    right, left = lax.rem(z + 1, n_mp), lax.rem(z + n_mp - 1, n_mp)
    for near in (left, right):
        pl.semaphore_signal(barrier, inc=1, device_id={"mp": near}, device_id_type=MESH)

    lanes = lax.broadcasted_iota(jnp.int32, (8, 128), 1)
    unit_of = jnp.zeros((8, 128), jnp.int32)
    place_of = jnp.zeros((8, 128), jnp.int32)
    for u in range(units):
        hit = lanes == server_ref[u]
        unit_of = jnp.where(hit, u, unit_of)
        place_of = jnp.where(hit, place_ref[u], place_of)
    inv_vec[...] = unit_of
    table_out[...] = place_of
    table_in[me] = place_of
    to_smem = pltpu.make_async_copy(inv_vec, inv_smem, small_sem.at[0])
    to_smem.start()
    to_smem.wait()

    pl.semaphore_wait(barrier, n_dp - 1 + 2)

    def mixed(i):
        return 1 + lax.rem(i * 11 + 5, n_dp - 1)

    def table_copy(o):
        to = peer(o)
        return pltpu.make_async_remote_copy(
            src_ref=table_out,
            dst_ref=table_in.at[me],
            send_sem=table_send.at[to],
            recv_sem=table_recv.at[me],
            device_id={"dp": to},
            device_id_type=MESH,
        )

    for p in range(count):
        for q, copy in loads:
            if p == q:
                copy.wait()

        def send_unit(i, carry, p=p):
            to = peer(mixed(i))
            stage[p][to] = held[p][inv_smem[0, to]]
            pltpu.make_async_remote_copy(
                src_ref=stage[p].at[to],
                dst_ref=recv[p].at[me],
                send_sem=a2a_send.at[p, to],
                recv_sem=a2a_recv.at[p, me],
                device_id={"dp": to},
                device_id_type=MESH,
            ).start()
            if p == 0:
                table_copy(mixed(i)).start()
            return carry

        lax.fori_loop(0, n_dp - 1, send_unit, 0)
        recv[p][me] = held[p][inv_smem[0, me]]
    for copy in weight_loads:
        copy.start()

    def table_arrived(o, carry):
        frm = peer(o)
        pltpu.make_async_remote_copy(
            src_ref=table_out,
            dst_ref=table_in.at[frm],
            send_sem=table_send.at[frm],
            recv_sem=table_recv.at[frm],
            device_id={"dp": frm},
            device_id_type=MESH,
        ).wait()
        return carry

    lax.fori_loop(1, n_dp, table_arrived, 0)
    table = table_in[:, 0, :]
    wide = lax.broadcasted_iota(jnp.int32, (units, 128), 1)
    tall = lax.broadcasted_iota(jnp.int32, (units, 128), 0)
    place_col = jnp.sum(jnp.where(wide == me, table, 0), axis=1, keepdims=True)
    source = jnp.max(jnp.where(place_col == wide, tall, 0), axis=0, keepdims=True)
    where_vec[pl.ds(0, units), :] = jnp.broadcast_to(place_col, (units, 128))
    where_vec[pl.ds(units, 8), :] = jnp.broadcast_to(source, (8, 128))
    to_smem = pltpu.make_async_copy(where_vec, where_smem, small_sem.at[1])
    to_smem.start()
    to_smem.wait()

    block = DOC_UNITS * unit_rows
    score_scale = 1.0 / math.sqrt(HEAD)
    exponent_scale = score_scale * math.log2(math.e)

    def one_doc(p, doc):
        length = length_ref[doc]
        sources = [where_smem[units, doc * DOC_UNITS + i] for i in range(DOC_UNITS)]

        def rows(p, at):
            return jnp.concatenate(
                [recv[p][s, :, pl.ds(at, HEAD)] for s in sources], axis=0
            )

        key_at = lax.broadcasted_iota(jnp.int32, (block, block), 0)
        query_at = lax.broadcasted_iota(jnp.int32, (block, block), 1)
        allowed = (key_at <= query_at) & (key_at < length)
        live = lax.broadcasted_iota(jnp.int32, (block, HEAD), 0) < length
        keys, values = rows(0, 0), rows(0, kv_cols)
        if p == 0:
            key_grad = jnp.zeros((block, HEAD), jnp.float32)
            value_grad = jnp.zeros((block, HEAD), jnp.float32)
        else:
            key_grad, value_grad = kv_total[doc, 0], kv_total[doc, 1]

        def store(at, value):
            low = value.astype(jnp.bfloat16)
            for i in range(DOC_UNITS):
                grads[doc * DOC_UNITS + i, :, pl.ds(at, HEAD)] = low[
                    i * unit_rows : (i + 1) * unit_rows
                ]

        for n, head in enumerate(phases[p]):
            at = 2 * n * HEAD + (0 if p else 2 * kv_cols)
            queries = rows(p, at)
            masked = rows(p, at + HEAD)
            masked = jnp.where(live, masked, jnp.zeros_like(masked))
            scores = jnp.where(allowed, dot(keys, queries, NT), -1e30)
            peak = jnp.max(scores, axis=0, keepdims=True)
            expanded = jnp.exp2((scores - peak) * exponent_scale)
            probs = expanded * (1.0 / jnp.sum(expanded, axis=0, keepdims=True))
            probs_low = probs.astype(jnp.bfloat16)
            prob_grad = dot(values, masked, NT)
            delta = jnp.sum(probs_low.astype(jnp.float32) * prob_grad, axis=0, keepdims=True)
            score_low = (probs * (prob_grad - delta)).astype(jnp.bfloat16)
            value_grad += dot(probs_low, masked, NN)
            key_grad += dot(score_low, queries, NN)
            store(head * HEAD, dot(score_low, keys, TN) * score_scale)
        if p == count - 1:
            store(q_cols, key_grad * score_scale)
            store(q_cols + kv_cols, value_grad)
        else:
            kv_total[doc, 0] = key_grad
            kv_total[doc, 1] = value_grad

    for p in range(count):

        def unit_arrived(o, carry, p=p):
            frm = peer(o)
            pltpu.make_async_remote_copy(
                src_ref=stage[p].at[frm],
                dst_ref=recv[p].at[frm],
                send_sem=a2a_send.at[p, frm],
                recv_sem=a2a_recv.at[p, frm],
                device_id={"dp": frm},
                device_id_type=MESH,
            ).wait()
            return carry

        lax.fori_loop(1, n_dp, unit_arrived, 0)

        def doc_phase(doc, carry, p=p):
            one_doc(p, doc)
            return carry

        lax.fori_loop(0, docs, doc_phase, 0)
    for copy in weight_loads:
        copy.wait()

    chunks = units // CHUNK_UNITS
    chunk_rows = CHUNK_UNITS * unit_rows
    half = chunk_rows // 2
    out_cols = out_hbm.shape[2]
    far = n_mp // 2

    def part(chunk, distance):
        column = lax.rem(z + distance, n_mp) * out_cols
        return dot(
            lhs[chunk],
            weights[pl.ds(pl.multiple_of(column, out_cols), out_cols), :],
            NT,
        )

    def ring_copy(chunk, way, step):
        first, count = (0, chunk_rows) if step else (way * half, half)
        return pltpu.make_async_remote_copy(
            src_ref=ring_send.at[chunk, way, step, pl.ds(first, count), :],
            dst_ref=ring_recv.at[chunk, way, step, pl.ds(first, count), :],
            send_sem=ring_send_sem.at[chunk, way, step],
            recv_sem=ring_recv_sem.at[chunk, way, step],
            device_id={"mp": left if way else right},
            device_id_type=MESH,
        )

    def back_copy(o):
        to = peer(o)
        return pltpu.make_async_remote_copy(
            src_ref=out_buf.at[o],
            dst_ref=out_hbm.at[me],
            send_sem=back_send.at[to],
            recv_sem=back_recv.at[me],
            device_id={"dp": to},
            device_id_type=MESH,
        )

    def first_step(chunk, carry):
        for i in range(CHUNK_UNITS):
            s = peer(chunk * CHUNK_UNITS + i)
            lhs[chunk, pl.ds(i * unit_rows, unit_rows), :] = grads[where_smem[s, 0]]
        low = part(chunk, far).astype(jnp.bfloat16)
        for way in range(2):
            ring_send[chunk, way, 0, pl.ds(way * half, half), :] = low[
                way * half : (way + 1) * half
            ]
            ring_copy(chunk, way, 0).start()
        return carry

    lax.fori_loop(0, chunks, first_step, 0)

    for step in range(1, far):

        def next_step(chunk, carry, step=step):
            for way in range(2):
                total = part(chunk, n_mp - far + step if way else far - step)
                ring_copy(chunk, way, step - 1).wait_recv()
                for h in range(2):
                    piece = total[h * half : (h + 1) * half]
                    if step > 1 or h == way:
                        piece += ring_recv[
                            chunk, way, step - 1, pl.ds(h * half, half), :
                        ].astype(jnp.float32)
                    ring_send[chunk, way, step, pl.ds(h * half, half), :] = piece.astype(
                        jnp.bfloat16
                    )
                ring_copy(chunk, way, step).start()
            return carry

        lax.fori_loop(0, chunks, next_step, 0)

    own_copy = pltpu.make_async_copy(out_buf.at[0], out_hbm.at[me], small_sem.at[2])

    def last_step(chunk, carry):
        total = part(chunk, 0)
        for way in range(2):
            ring_copy(chunk, way, far - 1).wait_recv()
            total += ring_recv[chunk, way, far - 1].astype(jnp.float32)
        low = total.astype(jnp.bfloat16)
        for i in range(CHUNK_UNITS):
            out_buf[chunk * CHUNK_UNITS + i] = low[i * unit_rows : (i + 1) * unit_rows]
        for i in range(CHUNK_UNITS):
            if i == 0:

                @pl.when(chunk == 0)
                def _():
                    own_copy.start()

                @pl.when(chunk > 0)
                def _():
                    back_copy(chunk * CHUNK_UNITS).start()
            else:
                back_copy(chunk * CHUNK_UNITS + i).start()
        return carry

    lax.fori_loop(0, chunks, last_step, 0)
    own_copy.wait()

    def ring_done(chunk, carry):
        for way in range(2):
            for step in range(far):
                ring_copy(chunk, way, step).wait_send()
        return carry

    lax.fori_loop(0, chunks, ring_done, 0)

    def back_arrived(o, carry):
        frm = peer(o)
        pltpu.make_async_remote_copy(
            src_ref=out_buf.at[o],
            dst_ref=out_hbm.at[frm],
            send_sem=back_send.at[frm],
            recv_sem=back_recv.at[frm],
            device_id={"dp": frm},
            device_id_type=MESH,
        ).wait()
        return carry

    lax.fori_loop(1, n_dp, back_arrived, 0)


def settle(server_ref, back_ref, out_ref):
    unit_rows = back_ref.shape[1]
    count = out_ref.shape[0] // unit_rows
    for i in range(count):
        u = pl.program_id(0) * count + i
        out_ref[pl.ds(i * unit_rows, unit_rows), :] = back_ref[server_ref[u]].astype(jnp.float32)


def local(
    saved_query,
    saved_key,
    saved_value,
    grad_output,
    unit_server,
    unit_place,
    doc_length,
    query_weight,
    key_weight,
    value_weight,
):
    n_dp, n_mp = lax.axis_size("dp"), lax.axis_size("mp")
    units = unit_server.shape[0]
    unit_rows = saved_query.shape[0] // units
    q_cols, kv_cols = saved_query.shape[1], saved_key.shape[1]
    out_all = query_weight.shape[0]
    out_cols = out_all // n_mp
    k_cols = q_cols + 2 * kv_cols
    heads = q_cols // HEAD
    phases = [range(0, heads - 2), range(heads - 2, heads - 1), range(heads - 1, heads)]
    widths = [2 * HEAD * len(p) for p in phases]
    widths[0] += 2 * kv_cols
    chunks = units // CHUNK_UNITS
    chunk_rows = CHUNK_UNITS * unit_rows
    far = n_mp // 2
    low = jnp.bfloat16

    def split(a):
        return a.reshape(units, unit_rows, a.shape[1])

    smem = pl.BlockSpec(memory_space=pltpu.SMEM)
    hbm = pl.BlockSpec(memory_space=pl.ANY)
    dma = pltpu.SemaphoreType.DMA
    back = pl.pallas_call(
        functools.partial(kernel, n_dp, n_mp, phases),
        out_shape=jax.ShapeDtypeStruct((n_dp, unit_rows, out_cols), low),
        in_specs=[smem] * 3 + [hbm] * 7,
        out_specs=hbm,
        scratch_shapes=[
            *[pltpu.VMEM((units, unit_rows, w), low) for w in widths],
            *[pltpu.VMEM((n_dp, unit_rows, w), low) for w in widths],
            *[pltpu.VMEM((n_dp, unit_rows, w), low) for w in widths],
            pltpu.VMEM((8, 128), jnp.int32),
            pltpu.VMEM((n_dp, 8, 128), jnp.int32),
            pltpu.VMEM((8, 128), jnp.int32),
            pltpu.SMEM((8, 128), jnp.int32),
            pltpu.VMEM((units + 8, 128), jnp.int32),
            pltpu.SMEM((units + 8, 128), jnp.int32),
            pltpu.VMEM((out_all, k_cols), low),
            pltpu.VMEM((units // DOC_UNITS, 2, DOC_UNITS * unit_rows, HEAD), jnp.float32),
            pltpu.VMEM((units, unit_rows, k_cols), low),
            pltpu.VMEM((chunks, chunk_rows, k_cols), low),
            pltpu.VMEM((chunks, 2, far, chunk_rows, out_cols), low),
            pltpu.VMEM((chunks, 2, far, chunk_rows, out_cols), low),
            pltpu.VMEM((units, unit_rows, out_cols), low),
            dma((2 + 2 * heads,)),
            dma((3,)),
            dma((3,)),
            dma((len(phases), n_dp)),
            dma((len(phases), n_dp)),
            dma((n_dp,)),
            dma((n_dp,)),
            dma((chunks, 2, far)),
            dma((chunks, 2, far)),
            dma((n_dp,)),
            dma((n_dp,)),
        ],
        compiler_params=pltpu.CompilerParams(
            collective_id=0, has_side_effects=True, vmem_limit_bytes=60 * 1024 * 1024
        ),
        name="attention_backward_exchange",
    )(
        unit_server,
        unit_place,
        doc_length,
        split(saved_query),
        split(saved_key),
        split(saved_value),
        split(grad_output),
        query_weight,
        key_weight,
        value_weight,
    )
    rows = units * unit_rows // SETTLE_STEPS
    return pl.pallas_call(
        settle,
        out_shape=jax.ShapeDtypeStruct((units * unit_rows, out_cols), jnp.float32),
        grid_spec=pltpu.PrefetchScalarGridSpec(
            num_scalar_prefetch=1,
            grid=(SETTLE_STEPS,),
            in_specs=[pl.BlockSpec(back.shape, lambda i, server: (0, 0, 0))],
            out_specs=pl.BlockSpec((rows, out_cols), lambda i, server: (i, 0)),
        ),
        name="settle_rows",
    )(unit_server, back)


def solution(mesh):
    placed = (
        P("dp", "mp"),
        P("dp", "mp"),
        P("dp", "mp"),
        P("dp", "mp"),
        P("dp"),
        P("dp"),
        P("dp"),
        P(None, "mp"),
        P(None, "mp"),
        P(None, "mp"),
    )
    return jax.shard_map(
        local, mesh=mesh, in_specs=placed, out_specs=P("dp", "mp"), check_vma=False
    )
```

```python
import functools
import math

import jax
import jax.numpy as jnp
from jax import lax
from jax.experimental import pallas as pl
from jax.experimental.pallas import tpu as pltpu
from jax.sharding import PartitionSpec as P

HEAD = 128
DOC_UNITS = 8
MESH = pl.DeviceIdType.MESH
NT = (((1,), (1,)), ((), ()))
NN = (((1,), (0,)), ((), ()))
TN = (((0,), (0,)), ((), ()))
CHUNK_UNITS = 4
SETTLE_STEPS = 4
GRID_Y, GRID_X, CORES = 4, 4, 2


def dot(a, b, numbers):
    return lax.dot_general(a, b, numbers, preferred_element_type=jnp.float32)


def kernel(
    n_dp,
    n_mp,
    phases,
    server_ref,
    place_ref,
    length_ref,
    q_hbm,
    k_hbm,
    v_hbm,
    g_hbm,
    wq_hbm,
    wk_hbm,
    wv_hbm,
    out_hbm,
    *scratch,
):
    count = len(phases)
    held, stage, recv = scratch[:count], scratch[count : 2 * count], scratch[2 * count : 3 * count]
    (
        table_out,
        table_in,
        inv_vec,
        inv_smem,
        where_vec,
        where_smem,
        weights,
        kv_total,
        grads,
        lhs,
        ring_send,
        ring_recv,
        out_buf,
        in_sem,
        weight_sem,
        small_sem,
        a2a_send,
        a2a_recv,
        table_send,
        table_recv,
        ring_send_sem,
        ring_recv_sem,
        back_send,
        back_recv,
    ) = scratch[3 * count :]
    me = lax.axis_index("dp")
    z = lax.axis_index("mp")
    units, unit_rows, q_cols = q_hbm.shape
    kv_cols = k_hbm.shape[2]
    docs = units // DOC_UNITS
    core = lax.rem(me, CORES)
    x = lax.rem(me // CORES, GRID_X)
    y = me // (CORES * GRID_X)

    def peer(offset):
        dc = lax.rem(offset, CORES)
        dx = lax.rem(offset // CORES, GRID_X)
        dy = offset // (CORES * GRID_X)
        return (
            lax.rem(y + dy, GRID_Y) * GRID_X + lax.rem(x + dx, GRID_X)
        ) * CORES + lax.rem(core + dc, CORES)

    loads = []
    for p, heads in enumerate(phases):
        pieces = [] if p else [(k_hbm, 0, kv_cols), (v_hbm, 0, kv_cols)]
        for head in heads:
            pieces += [(q_hbm, head * HEAD, HEAD), (g_hbm, head * HEAD, HEAD)]
        at = 0
        for n, (ref, first, width) in enumerate(pieces):
            loads.append(
                (
                    p,
                    pltpu.make_async_copy(
                        ref.at[:, :, pl.ds(first, width)],
                        held[p].at[:, :, pl.ds(at, width)],
                        in_sem.at[len(loads)],
                    ),
                )
            )
            at += width
    for _, copy in loads:
        copy.start()
    weight_loads = [
        pltpu.make_async_copy(wq_hbm, weights.at[:, pl.ds(0, q_cols)], weight_sem.at[0]),
        pltpu.make_async_copy(wk_hbm, weights.at[:, pl.ds(q_cols, kv_cols)], weight_sem.at[1]),
        pltpu.make_async_copy(
            wv_hbm, weights.at[:, pl.ds(q_cols + kv_cols, kv_cols)], weight_sem.at[2]
        ),
    ]

    barrier = pltpu.get_barrier_semaphore()

    def greet(o, carry):
        pl.semaphore_signal(barrier, inc=1, device_id={"dp": peer(o)}, device_id_type=MESH)
        return carry

    lax.fori_loop(1, n_dp, greet, 0)
    right, left = lax.rem(z + 1, n_mp), lax.rem(z + n_mp - 1, n_mp)
    for near in (left, right):
        pl.semaphore_signal(barrier, inc=1, device_id={"mp": near}, device_id_type=MESH)

    lanes = lax.broadcasted_iota(jnp.int32, (8, 128), 1)
    unit_of = jnp.zeros((8, 128), jnp.int32)
    place_of = jnp.zeros((8, 128), jnp.int32)
    for u in range(units):
        hit = lanes == server_ref[u]
        unit_of = jnp.where(hit, u, unit_of)
        place_of = jnp.where(hit, place_ref[u], place_of)
    inv_vec[...] = unit_of
    table_out[...] = place_of[:1]
    table_in[me] = place_of[:1]
    to_smem = pltpu.make_async_copy(inv_vec, inv_smem, small_sem.at[0])
    to_smem.start()
    to_smem.wait()

    pl.semaphore_wait(barrier, n_dp - 1 + 2)

    def mixed(i):
        return 1 + lax.rem(i * 11 + 5, n_dp - 1)

    def table_copy(o):
        to = peer(o)
        return pltpu.make_async_remote_copy(
            src_ref=table_out,
            dst_ref=table_in.at[me],
            send_sem=table_send.at[to],
            recv_sem=table_recv.at[me],
            device_id={"dp": to},
            device_id_type=MESH,
        )

    for p in range(count):
        for q, copy in loads:
            if p == q:
                copy.wait()

        def send_unit(i, carry, p=p):
            to = peer(mixed(i))
            stage[p][to] = held[p][inv_smem[0, to]]
            pltpu.make_async_remote_copy(
                src_ref=stage[p].at[to],
                dst_ref=recv[p].at[me],
                send_sem=a2a_send.at[p, to],
                recv_sem=a2a_recv.at[p, me],
                device_id={"dp": to},
                device_id_type=MESH,
            ).start()
            if p == 0:
                table_copy(mixed(i)).start()
            return carry

        lax.fori_loop(0, n_dp - 1, send_unit, 0)
        recv[p][me] = held[p][inv_smem[0, me]]
    for copy in weight_loads:
        copy.start()

    def table_arrived(o, carry):
        frm = peer(o)
        pltpu.make_async_remote_copy(
            src_ref=table_out,
            dst_ref=table_in.at[frm],
            send_sem=table_send.at[frm],
            recv_sem=table_recv.at[frm],
            device_id={"dp": frm},
            device_id_type=MESH,
        ).wait()
        return carry

    lax.fori_loop(1, n_dp, table_arrived, 0)
    table = table_in[:, 0, :]
    wide = lax.broadcasted_iota(jnp.int32, (units, 128), 1)
    tall = lax.broadcasted_iota(jnp.int32, (units, 128), 0)
    place_col = jnp.sum(jnp.where(wide == me, table, 0), axis=1, keepdims=True)
    source = jnp.max(jnp.where(place_col == wide, tall, 0), axis=0, keepdims=True)
    where_vec[pl.ds(0, units), :] = jnp.broadcast_to(place_col, (units, 128))
    where_vec[pl.ds(units, 8), :] = jnp.broadcast_to(source, (8, 128))
    to_smem = pltpu.make_async_copy(where_vec, where_smem, small_sem.at[1])
    to_smem.start()
    to_smem.wait()

    block = DOC_UNITS * unit_rows
    score_scale = 1.0 / math.sqrt(HEAD)
    exponent_scale = score_scale * math.log2(math.e)

    def one_doc(p, doc):
        length = length_ref[doc]
        sources = [where_smem[units, doc * DOC_UNITS + i] for i in range(DOC_UNITS)]

        def rows(p, at):
            return jnp.concatenate(
                [recv[p][s, :, pl.ds(at, HEAD)] for s in sources], axis=0
            )

        key_at = lax.broadcasted_iota(jnp.int32, (block, block), 0)
        query_at = lax.broadcasted_iota(jnp.int32, (block, block), 1)
        allowed = (key_at <= query_at) & (key_at < length)
        live = lax.broadcasted_iota(jnp.int32, (block, HEAD), 0) < length
        keys, values = rows(0, 0), rows(0, kv_cols)
        if p == 0:
            key_grad = jnp.zeros((block, HEAD), jnp.float32)
            value_grad = jnp.zeros((block, HEAD), jnp.float32)
        else:
            key_grad, value_grad = kv_total[doc, 0], kv_total[doc, 1]

        def store(at, value):
            low = value.astype(jnp.bfloat16)
            for i in range(DOC_UNITS):
                grads[doc * DOC_UNITS + i, :, pl.ds(at, HEAD)] = low[
                    i * unit_rows : (i + 1) * unit_rows
                ]

        for n, head in enumerate(phases[p]):
            at = 2 * n * HEAD + (0 if p else 2 * kv_cols)
            queries = rows(p, at)
            masked = rows(p, at + HEAD)
            masked = jnp.where(live, masked, jnp.zeros_like(masked))
            scores = jnp.where(allowed, dot(keys, queries, NT), -1e30)
            peak = jnp.max(scores, axis=0, keepdims=True)
            expanded = jnp.exp2((scores - peak) * exponent_scale)
            probs = expanded * (1.0 / jnp.sum(expanded, axis=0, keepdims=True))
            probs_low = probs.astype(jnp.bfloat16)
            prob_grad = dot(values, masked, NT)
            delta = jnp.sum(probs_low.astype(jnp.float32) * prob_grad, axis=0, keepdims=True)
            score_low = (probs * (prob_grad - delta)).astype(jnp.bfloat16)
            value_grad += dot(probs_low, masked, NN)
            key_grad += dot(score_low, queries, NN)
            store(head * HEAD, dot(score_low, keys, TN) * score_scale)
        if p == count - 1:
            store(q_cols, key_grad * score_scale)
            store(q_cols + kv_cols, value_grad)
        else:
            kv_total[doc, 0] = key_grad
            kv_total[doc, 1] = value_grad

    for p in range(count):

        def unit_arrived(o, carry, p=p):
            frm = peer(o)
            pltpu.make_async_remote_copy(
                src_ref=stage[p].at[frm],
                dst_ref=recv[p].at[frm],
                send_sem=a2a_send.at[p, frm],
                recv_sem=a2a_recv.at[p, frm],
                device_id={"dp": frm},
                device_id_type=MESH,
            ).wait()
            return carry

        lax.fori_loop(1, n_dp, unit_arrived, 0)

        def doc_phase(doc, carry, p=p):
            one_doc(p, doc)
            return carry

        lax.fori_loop(0, docs, doc_phase, 0)
    for copy in weight_loads:
        copy.wait()

    chunks = units // CHUNK_UNITS
    chunk_rows = CHUNK_UNITS * unit_rows
    half = chunk_rows // 2
    out_cols = out_hbm.shape[2]
    far = n_mp // 2

    def part(chunk, distance):
        column = lax.rem(z + distance, n_mp) * out_cols
        return dot(
            lhs[chunk],
            weights[pl.ds(pl.multiple_of(column, out_cols), out_cols), :],
            NT,
        )

    def ring_copy(chunk, way, step):
        first, count = (0, chunk_rows) if step else (way * half, half)
        return pltpu.make_async_remote_copy(
            src_ref=ring_send.at[chunk, way, step, pl.ds(first, count), :],
            dst_ref=ring_recv.at[chunk, way, step, pl.ds(first, count), :],
            send_sem=ring_send_sem.at[chunk, way, step],
            recv_sem=ring_recv_sem.at[chunk, way, step],
            device_id={"mp": left if way else right},
            device_id_type=MESH,
        )

    def back_copy(o):
        to = peer(n_dp - 1 - o)
        return pltpu.make_async_remote_copy(
            src_ref=out_buf.at[o],
            dst_ref=out_hbm.at[me],
            send_sem=back_send.at[to],
            recv_sem=back_recv.at[me],
            device_id={"dp": to},
            device_id_type=MESH,
        )

    def first_step(chunk, carry):
        for i in range(CHUNK_UNITS):
            s = peer(n_dp - 1 - (chunk * CHUNK_UNITS + i))
            lhs[chunk, pl.ds(i * unit_rows, unit_rows), :] = grads[where_smem[s, 0]]
        low = part(chunk, far).astype(jnp.bfloat16)
        for way in range(2):
            ring_send[chunk, way, 0, pl.ds(way * half, half), :] = low[
                way * half : (way + 1) * half
            ]
            ring_copy(chunk, way, 0).start()
        return carry

    lax.fori_loop(0, chunks, first_step, 0)

    for step in range(1, far):

        def next_step(chunk, carry, step=step):
            for way in range(2):
                total = part(chunk, n_mp - far + step if way else far - step)
                ring_copy(chunk, way, step - 1).wait_recv()
                for h in range(2):
                    piece = total[h * half : (h + 1) * half]
                    if step > 1 or h == way:
                        piece += ring_recv[
                            chunk, way, step - 1, pl.ds(h * half, half), :
                        ].astype(jnp.float32)
                    ring_send[chunk, way, step, pl.ds(h * half, half), :] = piece.astype(
                        jnp.bfloat16
                    )
                ring_copy(chunk, way, step).start()
            return carry

        lax.fori_loop(0, chunks, next_step, 0)

    own_copy = pltpu.make_async_copy(out_buf.at[n_dp - 1], out_hbm.at[me], small_sem.at[2])

    def last_step(chunk, carry):
        total = part(chunk, 0)
        for way in range(2):
            ring_copy(chunk, way, far - 1).wait_recv()
            total += ring_recv[chunk, way, far - 1].astype(jnp.float32)
        low = total.astype(jnp.bfloat16)
        for i in range(CHUNK_UNITS):
            out_buf[chunk * CHUNK_UNITS + i] = low[i * unit_rows : (i + 1) * unit_rows]
        for i in range(CHUNK_UNITS - 1):
            back_copy(chunk * CHUNK_UNITS + i).start()

        @pl.when(chunk < chunks - 1)
        def _():
            back_copy(chunk * CHUNK_UNITS + CHUNK_UNITS - 1).start()

        @pl.when(chunk == chunks - 1)
        def _():
            own_copy.start()

        return carry

    lax.fori_loop(0, chunks, last_step, 0)
    own_copy.wait()

    def ring_done(chunk, carry):
        for way in range(2):
            for step in range(far):
                ring_copy(chunk, way, step).wait_send()
        return carry

    lax.fori_loop(0, chunks, ring_done, 0)

    def back_arrived(o, carry):
        frm = peer(o)
        pltpu.make_async_remote_copy(
            src_ref=out_buf.at[o],
            dst_ref=out_hbm.at[frm],
            send_sem=back_send.at[frm],
            recv_sem=back_recv.at[frm],
            device_id={"dp": frm},
            device_id_type=MESH,
        ).wait()
        return carry

    lax.fori_loop(1, n_dp, back_arrived, 0)


def settle(server_ref, back_hbm, out_hbm, held, wide, in_sem, out_sem):
    units, unit_rows = held.shape[:2]
    rows = units * unit_rows // SETTLE_STEPS

    def fetch(u):
        return pltpu.make_async_copy(back_hbm.at[server_ref[u]], held.at[u], in_sem.at[u])

    def emit(step):
        part = pl.ds(step * rows, rows)
        return pltpu.make_async_copy(wide.at[part, :], out_hbm.at[part, :], out_sem.at[step])

    for u in range(units):
        fetch(u).start()
    for step in range(SETTLE_STEPS):
        for u in range(step * units // SETTLE_STEPS, (step + 1) * units // SETTLE_STEPS):
            fetch(u).wait()
            wide[pl.ds(u * unit_rows, unit_rows), :] = held[u].astype(jnp.float32)
        emit(step).start()
    for step in range(SETTLE_STEPS):
        emit(step).wait()


def local(
    saved_query,
    saved_key,
    saved_value,
    grad_output,
    unit_server,
    unit_place,
    doc_length,
    query_weight,
    key_weight,
    value_weight,
):
    n_dp, n_mp = lax.axis_size("dp"), lax.axis_size("mp")
    units = unit_server.shape[0]
    unit_rows = saved_query.shape[0] // units
    q_cols, kv_cols = saved_query.shape[1], saved_key.shape[1]
    out_all = query_weight.shape[0]
    out_cols = out_all // n_mp
    k_cols = q_cols + 2 * kv_cols
    heads = q_cols // HEAD
    phases = [range(0, heads - 2), range(heads - 2, heads - 1), range(heads - 1, heads)]
    widths = [2 * HEAD * len(p) for p in phases]
    widths[0] += 2 * kv_cols
    chunks = units // CHUNK_UNITS
    chunk_rows = CHUNK_UNITS * unit_rows
    far = n_mp // 2
    low = jnp.bfloat16

    def split(a):
        return a.reshape(units, unit_rows, a.shape[1])

    smem = pl.BlockSpec(memory_space=pltpu.SMEM)
    hbm = pl.BlockSpec(memory_space=pl.ANY)
    dma = pltpu.SemaphoreType.DMA
    back = pl.pallas_call(
        functools.partial(kernel, n_dp, n_mp, phases),
        out_shape=jax.ShapeDtypeStruct((n_dp, unit_rows, out_cols), low),
        in_specs=[smem] * 3 + [hbm] * 7,
        out_specs=hbm,
        scratch_shapes=[
            *[pltpu.VMEM((units, unit_rows, w), low) for w in widths],
            *[pltpu.VMEM((n_dp, unit_rows, w), low) for w in widths],
            *[pltpu.VMEM((n_dp, unit_rows, w), low) for w in widths],
            pltpu.VMEM((1, 128), jnp.int32),
            pltpu.VMEM((n_dp, 1, 128), jnp.int32),
            pltpu.VMEM((8, 128), jnp.int32),
            pltpu.SMEM((8, 128), jnp.int32),
            pltpu.VMEM((units + 8, 128), jnp.int32),
            pltpu.SMEM((units + 8, 128), jnp.int32),
            pltpu.VMEM((out_all, k_cols), low),
            pltpu.VMEM((units // DOC_UNITS, 2, DOC_UNITS * unit_rows, HEAD), jnp.float32),
            pltpu.VMEM((units, unit_rows, k_cols), low),
            pltpu.VMEM((chunks, chunk_rows, k_cols), low),
            pltpu.VMEM((chunks, 2, far, chunk_rows, out_cols), low),
            pltpu.VMEM((chunks, 2, far, chunk_rows, out_cols), low),
            pltpu.VMEM((units, unit_rows, out_cols), low),
            dma((2 + 2 * heads,)),
            dma((3,)),
            dma((3,)),
            dma((len(phases), n_dp)),
            dma((len(phases), n_dp)),
            dma((n_dp,)),
            dma((n_dp,)),
            dma((chunks, 2, far)),
            dma((chunks, 2, far)),
            dma((n_dp,)),
            dma((n_dp,)),
        ],
        compiler_params=pltpu.CompilerParams(
            collective_id=0, has_side_effects=True, vmem_limit_bytes=60 * 1024 * 1024
        ),
        name="attention_backward_exchange",
    )(
        unit_server,
        unit_place,
        doc_length,
        split(saved_query),
        split(saved_key),
        split(saved_value),
        split(grad_output),
        query_weight,
        key_weight,
        value_weight,
    )
    return pl.pallas_call(
        settle,
        out_shape=jax.ShapeDtypeStruct((units * unit_rows, out_cols), jnp.float32),
        in_specs=[smem, hbm],
        out_specs=hbm,
        scratch_shapes=[
            pltpu.VMEM((units, unit_rows, out_cols), low),
            pltpu.VMEM((units * unit_rows, out_cols), jnp.float32),
            dma((units,)),
            dma((SETTLE_STEPS,)),
        ],
        name="settle_rows",
    )(unit_server, back)


def solution(mesh):
    placed = (
        P("dp", "mp"),
        P("dp", "mp"),
        P("dp", "mp"),
        P("dp", "mp"),
        P("dp"),
        P("dp"),
        P("dp"),
        P(None, "mp"),
        P(None, "mp"),
        P(None, "mp"),
    )
    return jax.shard_map(
        local, mesh=mesh, in_specs=placed, out_specs=P("dp", "mp"), check_vma=False
    )
```

```python
import functools
import math

import jax
import jax.numpy as jnp
from jax import lax
from jax.experimental import pallas as pl
from jax.experimental.pallas import tpu as pltpu
from jax.sharding import PartitionSpec as P

HEAD = 128
DOC_UNITS = 8
MESH = pl.DeviceIdType.MESH
NT = (((1,), (1,)), ((), ()))
NN = (((1,), (0,)), ((), ()))
TN = (((0,), (0,)), ((), ()))
CHUNK_UNITS = 4
SETTLE_STEPS = 4
GRID_Y, GRID_X, CORES = 4, 4, 2
ORDER_STRIDE, ORDER_START = 7, 3


def dot(a, b, numbers):
    return lax.dot_general(a, b, numbers, preferred_element_type=jnp.float32)


def kernel(
    n_dp,
    n_mp,
    phases,
    server_ref,
    place_ref,
    length_ref,
    q_hbm,
    k_hbm,
    v_hbm,
    g_hbm,
    wq_hbm,
    wk_hbm,
    wv_hbm,
    out_hbm,
    *scratch,
):
    count = len(phases)
    held, stage, recv = scratch[:count], scratch[count : 2 * count], scratch[2 * count : 3 * count]
    (
        table_out,
        table_in,
        inv_vec,
        inv_smem,
        where_vec,
        where_smem,
        weights,
        kv_total,
        grads,
        lhs,
        ring_send,
        ring_recv,
        out_buf,
        in_sem,
        weight_sem,
        small_sem,
        a2a_send,
        a2a_recv,
        table_send,
        table_recv,
        ring_send_sem,
        ring_recv_sem,
        back_send,
        back_recv,
    ) = scratch[3 * count :]
    me = lax.axis_index("dp")
    z = lax.axis_index("mp")
    units, unit_rows, q_cols = q_hbm.shape
    kv_cols = k_hbm.shape[2]
    docs = units // DOC_UNITS
    core = lax.rem(me, CORES)
    x = lax.rem(me // CORES, GRID_X)
    y = me // (CORES * GRID_X)

    def peer(offset):
        dc = lax.rem(offset, CORES)
        dx = lax.rem(offset // CORES, GRID_X)
        dy = offset // (CORES * GRID_X)
        return (
            lax.rem(y + dy, GRID_Y) * GRID_X + lax.rem(x + dx, GRID_X)
        ) * CORES + lax.rem(core + dc, CORES)

    loads = []
    for p, heads in enumerate(phases):
        pieces = [] if p else [(k_hbm, 0, kv_cols), (v_hbm, 0, kv_cols)]
        for head in heads:
            pieces += [(q_hbm, head * HEAD, HEAD), (g_hbm, head * HEAD, HEAD)]
        at = 0
        for n, (ref, first, width) in enumerate(pieces):
            loads.append(
                (
                    p,
                    pltpu.make_async_copy(
                        ref.at[:, :, pl.ds(first, width)],
                        held[p].at[:, :, pl.ds(at, width)],
                        in_sem.at[len(loads)],
                    ),
                )
            )
            at += width
    for _, copy in loads:
        copy.start()
    weight_loads = [
        pltpu.make_async_copy(wq_hbm, weights.at[:, pl.ds(0, q_cols)], weight_sem.at[0]),
        pltpu.make_async_copy(wk_hbm, weights.at[:, pl.ds(q_cols, kv_cols)], weight_sem.at[1]),
        pltpu.make_async_copy(
            wv_hbm, weights.at[:, pl.ds(q_cols + kv_cols, kv_cols)], weight_sem.at[2]
        ),
    ]

    barrier = pltpu.get_barrier_semaphore()

    def greet(o, carry):
        pl.semaphore_signal(barrier, inc=1, device_id={"dp": peer(o)}, device_id_type=MESH)
        return carry

    lax.fori_loop(1, n_dp, greet, 0)
    right, left = lax.rem(z + 1, n_mp), lax.rem(z + n_mp - 1, n_mp)
    for near in (left, right):
        pl.semaphore_signal(barrier, inc=1, device_id={"mp": near}, device_id_type=MESH)

    lanes = lax.broadcasted_iota(jnp.int32, (8, 128), 1)
    unit_of = jnp.zeros((8, 128), jnp.int32)
    place_of = jnp.zeros((8, 128), jnp.int32)
    for u in range(units):
        hit = lanes == server_ref[u]
        unit_of = jnp.where(hit, u, unit_of)
        place_of = jnp.where(hit, place_ref[u], place_of)
    inv_vec[...] = unit_of
    table_out[...] = place_of[:1]
    table_in[me] = place_of[:1]
    to_smem = pltpu.make_async_copy(inv_vec, inv_smem, small_sem.at[0])
    to_smem.start()
    to_smem.wait()

    pl.semaphore_wait(barrier, n_dp - 1 + 2)

    def chip_peer(i, to_core):
        j = lax.rem(i * ORDER_STRIDE + ORDER_START, GRID_X * GRID_Y)
        dx = lax.rem(j, GRID_X)
        dy = j // GRID_X
        return (
            lax.rem(y + dy, GRID_Y) * GRID_X + lax.rem(x + dx, GRID_X)
        ) * CORES + to_core

    for to_core in range(CORES):
        for p in range(count):
            if to_core == 0:
                for q, copy in loads:
                    if p == q:
                        copy.wait()
                recv[p][me] = held[p][inv_smem[0, me]]

            def send_unit(i, carry, p=p, to_core=to_core):
                to = chip_peer(i, to_core)

                @pl.when(to != me)
                def _():
                    stage[p][to] = held[p][inv_smem[0, to]]
                    pltpu.make_async_remote_copy(
                        src_ref=stage[p].at[to],
                        dst_ref=recv[p].at[me],
                        send_sem=a2a_send.at[p, to],
                        recv_sem=a2a_recv.at[p, me],
                        device_id={"dp": to},
                        device_id_type=MESH,
                    ).start()
                    if p == 0:
                        pltpu.make_async_remote_copy(
                            src_ref=table_out,
                            dst_ref=table_in.at[me],
                            send_sem=table_send.at[to],
                            recv_sem=table_recv.at[me],
                            device_id={"dp": to},
                            device_id_type=MESH,
                        ).start()

                return carry

            lax.fori_loop(0, GRID_X * GRID_Y, send_unit, 0)
    for copy in weight_loads:
        copy.start()

    def table_arrived(o, carry):
        frm = peer(o)
        pltpu.make_async_remote_copy(
            src_ref=table_out,
            dst_ref=table_in.at[frm],
            send_sem=table_send.at[frm],
            recv_sem=table_recv.at[frm],
            device_id={"dp": frm},
            device_id_type=MESH,
        ).wait_recv()
        return carry

    lax.fori_loop(1, n_dp, table_arrived, 0)
    table = table_in[:, 0, :]
    wide = lax.broadcasted_iota(jnp.int32, (units, 128), 1)
    tall = lax.broadcasted_iota(jnp.int32, (units, 128), 0)
    place_col = jnp.sum(jnp.where(wide == me, table, 0), axis=1, keepdims=True)
    source = jnp.max(jnp.where(place_col == wide, tall, 0), axis=0, keepdims=True)
    where_vec[pl.ds(0, units), :] = jnp.broadcast_to(place_col, (units, 128))
    where_vec[pl.ds(units, 8), :] = jnp.broadcast_to(source, (8, 128))
    to_smem = pltpu.make_async_copy(where_vec, where_smem, small_sem.at[1])
    to_smem.start()
    to_smem.wait()

    block = DOC_UNITS * unit_rows
    score_scale = 1.0 / math.sqrt(HEAD)
    exponent_scale = score_scale * math.log2(math.e)

    def one_doc(p, doc):
        length = length_ref[doc]
        sources = [where_smem[units, doc * DOC_UNITS + i] for i in range(DOC_UNITS)]

        def rows(p, at):
            return jnp.concatenate(
                [recv[p][s, :, pl.ds(at, HEAD)] for s in sources], axis=0
            )

        key_at = lax.broadcasted_iota(jnp.int32, (block, block), 0)
        query_at = lax.broadcasted_iota(jnp.int32, (block, block), 1)
        allowed = (key_at <= query_at) & (key_at < length)
        live = lax.broadcasted_iota(jnp.int32, (block, HEAD), 0) < length
        keys, values = rows(0, 0), rows(0, kv_cols)
        if p == 0:
            key_grad = jnp.zeros((block, HEAD), jnp.float32)
            value_grad = jnp.zeros((block, HEAD), jnp.float32)
        else:
            key_grad, value_grad = kv_total[doc, 0], kv_total[doc, 1]

        def store(at, value):
            low = value.astype(jnp.bfloat16)
            for i in range(DOC_UNITS):
                grads[doc * DOC_UNITS + i, :, pl.ds(at, HEAD)] = low[
                    i * unit_rows : (i + 1) * unit_rows
                ]

        for n, head in enumerate(phases[p]):
            at = 2 * n * HEAD + (0 if p else 2 * kv_cols)
            queries = rows(p, at)
            masked = rows(p, at + HEAD)
            masked = jnp.where(live, masked, jnp.zeros_like(masked))
            scores = jnp.where(allowed, dot(keys, queries, NT), -1e30)
            peak = jnp.max(scores, axis=0, keepdims=True)
            expanded = jnp.exp2((scores - peak) * exponent_scale)
            probs = expanded * (1.0 / jnp.sum(expanded, axis=0, keepdims=True))
            probs_low = probs.astype(jnp.bfloat16)
            prob_grad = dot(values, masked, NT)
            delta = jnp.sum(probs_low.astype(jnp.float32) * prob_grad, axis=0, keepdims=True)
            score_low = (probs * (prob_grad - delta)).astype(jnp.bfloat16)
            value_grad += dot(probs_low, masked, NN)
            key_grad += dot(score_low, queries, NN)
            store(head * HEAD, dot(score_low, keys, TN) * score_scale)
        if p == count - 1:
            store(q_cols, key_grad * score_scale)
            store(q_cols + kv_cols, value_grad)
        else:
            kv_total[doc, 0] = key_grad
            kv_total[doc, 1] = value_grad

    def unit_copy(p, frm):
        return pltpu.make_async_remote_copy(
            src_ref=stage[p].at[frm],
            dst_ref=recv[p].at[frm],
            send_sem=a2a_send.at[p, frm],
            recv_sem=a2a_recv.at[p, frm],
            device_id={"dp": frm},
            device_id_type=MESH,
        )

    for p in range(count):

        def unit_arrived(o, carry, p=p):
            unit_copy(p, peer(o)).wait_recv()
            return carry

        lax.fori_loop(1, n_dp, unit_arrived, 0)

        def doc_phase(doc, carry, p=p):
            one_doc(p, doc)
            return carry

        lax.fori_loop(0, docs, doc_phase, 0)
    for copy in weight_loads:
        copy.wait()

    chunks = units // CHUNK_UNITS
    chunk_rows = CHUNK_UNITS * unit_rows
    half = chunk_rows // 2
    out_cols = out_hbm.shape[2]
    far = n_mp // 2

    def part(chunk, distance):
        column = lax.rem(z + distance, n_mp) * out_cols
        return dot(
            lhs[chunk],
            weights[pl.ds(pl.multiple_of(column, out_cols), out_cols), :],
            NT,
        )

    def ring_copy(chunk, way, step):
        first, count = (0, chunk_rows) if step else (way * half, half)
        return pltpu.make_async_remote_copy(
            src_ref=ring_send.at[chunk, way, step, pl.ds(first, count), :],
            dst_ref=ring_recv.at[chunk, way, step, pl.ds(first, count), :],
            send_sem=ring_send_sem.at[chunk, way, step],
            recv_sem=ring_recv_sem.at[chunk, way, step],
            device_id={"mp": left if way else right},
            device_id_type=MESH,
        )

    def back_copy(o):
        to = peer(n_dp - 1 - o)
        return pltpu.make_async_remote_copy(
            src_ref=out_buf.at[o],
            dst_ref=out_hbm.at[me],
            send_sem=back_send.at[to],
            recv_sem=back_recv.at[me],
            device_id={"dp": to},
            device_id_type=MESH,
        )

    def first_step(chunk, carry):
        for i in range(CHUNK_UNITS):
            s = peer(n_dp - 1 - (chunk * CHUNK_UNITS + i))
            lhs[chunk, pl.ds(i * unit_rows, unit_rows), :] = grads[where_smem[s, 0]]
        low = part(chunk, far).astype(jnp.bfloat16)
        for way in range(2):
            ring_send[chunk, way, 0, pl.ds(way * half, half), :] = low[
                way * half : (way + 1) * half
            ]
            ring_copy(chunk, way, 0).start()
        return carry

    lax.fori_loop(0, chunks, first_step, 0)

    for step in range(1, far):

        def next_step(chunk, carry, step=step):
            for way in range(2):
                total = part(chunk, n_mp - far + step if way else far - step)
                ring_copy(chunk, way, step - 1).wait_recv()
                for h in range(2):
                    piece = total[h * half : (h + 1) * half]
                    if step > 1 or h == way:
                        piece += ring_recv[
                            chunk, way, step - 1, pl.ds(h * half, half), :
                        ].astype(jnp.float32)
                    ring_send[chunk, way, step, pl.ds(h * half, half), :] = piece.astype(
                        jnp.bfloat16
                    )
                ring_copy(chunk, way, step).start()
            return carry

        lax.fori_loop(0, chunks, next_step, 0)

    own_copy = pltpu.make_async_copy(out_buf.at[n_dp - 1], out_hbm.at[me], small_sem.at[2])

    def last_step(chunk, carry):
        total = part(chunk, 0)
        for way in range(2):
            ring_copy(chunk, way, far - 1).wait_recv()
            total += ring_recv[chunk, way, far - 1].astype(jnp.float32)
        low = total.astype(jnp.bfloat16)
        for i in range(CHUNK_UNITS):
            out_buf[chunk * CHUNK_UNITS + i] = low[i * unit_rows : (i + 1) * unit_rows]
        for i in range(CHUNK_UNITS - 1):
            back_copy(chunk * CHUNK_UNITS + i).start()

        @pl.when(chunk < chunks - 1)
        def _():
            back_copy(chunk * CHUNK_UNITS + CHUNK_UNITS - 1).start()

        @pl.when(chunk == chunks - 1)
        def _():
            own_copy.start()

        return carry

    lax.fori_loop(0, chunks, last_step, 0)
    own_copy.wait()

    def exchange_done(o, carry):
        to = peer(o)
        pltpu.make_async_remote_copy(
            src_ref=table_out,
            dst_ref=table_in.at[to],
            send_sem=table_send.at[to],
            recv_sem=table_recv.at[to],
            device_id={"dp": to},
            device_id_type=MESH,
        ).wait_send()
        for p in range(count):
            unit_copy(p, to).wait_send()
        return carry

    lax.fori_loop(1, n_dp, exchange_done, 0)

    def ring_done(chunk, carry):
        for way in range(2):
            for step in range(far):
                ring_copy(chunk, way, step).wait_send()
        return carry

    lax.fori_loop(0, chunks, ring_done, 0)

    def back_arrived(o, carry):
        frm = peer(o)
        pltpu.make_async_remote_copy(
            src_ref=out_buf.at[o],
            dst_ref=out_hbm.at[frm],
            send_sem=back_send.at[frm],
            recv_sem=back_recv.at[frm],
            device_id={"dp": frm},
            device_id_type=MESH,
        ).wait()
        return carry

    lax.fori_loop(1, n_dp, back_arrived, 0)


def settle(server_ref, back_hbm, out_hbm, held, wide, in_sem, out_sem):
    units, unit_rows = held.shape[:2]
    rows = units * unit_rows // SETTLE_STEPS

    def fetch(u):
        return pltpu.make_async_copy(back_hbm.at[server_ref[u]], held.at[u], in_sem.at[u])

    def emit(step):
        part = pl.ds(step * rows, rows)
        return pltpu.make_async_copy(wide.at[part, :], out_hbm.at[part, :], out_sem.at[step])

    for u in range(units):
        fetch(u).start()
    for step in range(SETTLE_STEPS):
        for u in range(step * units // SETTLE_STEPS, (step + 1) * units // SETTLE_STEPS):
            fetch(u).wait()
            wide[pl.ds(u * unit_rows, unit_rows), :] = held[u].astype(jnp.float32)
        emit(step).start()
    for step in range(SETTLE_STEPS):
        emit(step).wait()


def local(
    saved_query,
    saved_key,
    saved_value,
    grad_output,
    unit_server,
    unit_place,
    doc_length,
    query_weight,
    key_weight,
    value_weight,
):
    n_dp, n_mp = lax.axis_size("dp"), lax.axis_size("mp")
    units = unit_server.shape[0]
    unit_rows = saved_query.shape[0] // units
    q_cols, kv_cols = saved_query.shape[1], saved_key.shape[1]
    out_all = query_weight.shape[0]
    out_cols = out_all // n_mp
    k_cols = q_cols + 2 * kv_cols
    heads = q_cols // HEAD
    phases = [range(0, heads - 2), range(heads - 2, heads - 1), range(heads - 1, heads)]
    widths = [2 * HEAD * len(p) for p in phases]
    widths[0] += 2 * kv_cols
    chunks = units // CHUNK_UNITS
    chunk_rows = CHUNK_UNITS * unit_rows
    far = n_mp // 2
    low = jnp.bfloat16

    def split(a):
        return a.reshape(units, unit_rows, a.shape[1])

    smem = pl.BlockSpec(memory_space=pltpu.SMEM)
    hbm = pl.BlockSpec(memory_space=pl.ANY)
    dma = pltpu.SemaphoreType.DMA
    back = pl.pallas_call(
        functools.partial(kernel, n_dp, n_mp, phases),
        out_shape=jax.ShapeDtypeStruct((n_dp, unit_rows, out_cols), low),
        in_specs=[smem] * 3 + [hbm] * 7,
        out_specs=hbm,
        scratch_shapes=[
            *[pltpu.VMEM((units, unit_rows, w), low) for w in widths],
            *[pltpu.VMEM((n_dp, unit_rows, w), low) for w in widths],
            *[pltpu.VMEM((n_dp, unit_rows, w), low) for w in widths],
            pltpu.VMEM((1, 128), jnp.int32),
            pltpu.VMEM((n_dp, 1, 128), jnp.int32),
            pltpu.VMEM((8, 128), jnp.int32),
            pltpu.SMEM((8, 128), jnp.int32),
            pltpu.VMEM((units + 8, 128), jnp.int32),
            pltpu.SMEM((units + 8, 128), jnp.int32),
            pltpu.VMEM((out_all, k_cols), low),
            pltpu.VMEM((units // DOC_UNITS, 2, DOC_UNITS * unit_rows, HEAD), jnp.float32),
            pltpu.VMEM((units, unit_rows, k_cols), low),
            pltpu.VMEM((chunks, chunk_rows, k_cols), low),
            pltpu.VMEM((chunks, 2, far, chunk_rows, out_cols), low),
            pltpu.VMEM((chunks, 2, far, chunk_rows, out_cols), low),
            pltpu.VMEM((units, unit_rows, out_cols), low),
            dma((2 + 2 * heads,)),
            dma((3,)),
            dma((3,)),
            dma((len(phases), n_dp)),
            dma((len(phases), n_dp)),
            dma((n_dp,)),
            dma((n_dp,)),
            dma((chunks, 2, far)),
            dma((chunks, 2, far)),
            dma((n_dp,)),
            dma((n_dp,)),
        ],
        compiler_params=pltpu.CompilerParams(
            collective_id=0, has_side_effects=True, vmem_limit_bytes=60 * 1024 * 1024
        ),
        name="attention_backward_exchange",
    )(
        unit_server,
        unit_place,
        doc_length,
        split(saved_query),
        split(saved_key),
        split(saved_value),
        split(grad_output),
        query_weight,
        key_weight,
        value_weight,
    )
    return pl.pallas_call(
        settle,
        out_shape=jax.ShapeDtypeStruct((units * unit_rows, out_cols), jnp.float32),
        in_specs=[smem, hbm],
        out_specs=hbm,
        scratch_shapes=[
            pltpu.VMEM((units, unit_rows, out_cols), low),
            pltpu.VMEM((units * unit_rows, out_cols), jnp.float32),
            dma((units,)),
            dma((SETTLE_STEPS,)),
        ],
        name="settle_rows",
    )(unit_server, back)


def solution(mesh):
    placed = (
        P("dp", "mp"),
        P("dp", "mp"),
        P("dp", "mp"),
        P("dp", "mp"),
        P("dp"),
        P("dp"),
        P("dp"),
        P(None, "mp"),
        P(None, "mp"),
        P(None, "mp"),
    )
    return jax.shard_map(
        local, mesh=mesh, in_specs=placed, out_specs=P("dp", "mp"), check_vma=False
    )
```

```python
import functools
import math

import jax
import jax.numpy as jnp
from jax import lax
from jax.experimental import pallas as pl
from jax.experimental.pallas import tpu as pltpu
from jax.sharding import PartitionSpec as P

HEAD = 128
DOC_UNITS = 8
MESH = pl.DeviceIdType.MESH
NT = (((1,), (1,)), ((), ()))
NN = (((1,), (0,)), ((), ()))
TN = (((0,), (0,)), ((), ()))
CHUNK_UNITS = 4
SETTLE_STEPS = 4
GRID_Y, GRID_X, CORES = 4, 4, 2
ORDER_STRIDE, ORDER_START = 7, 3


def dot(a, b, numbers):
    return lax.dot_general(a, b, numbers, preferred_element_type=jnp.float32)


def kernel(
    n_dp,
    n_mp,
    phases,
    server_ref,
    place_ref,
    length_ref,
    q_hbm,
    k_hbm,
    v_hbm,
    g_hbm,
    wq_hbm,
    wk_hbm,
    wv_hbm,
    out_hbm,
    *scratch,
):
    count = len(phases)
    held, stage, recv = scratch[:count], scratch[count : 2 * count], scratch[2 * count : 3 * count]
    (
        table_out,
        table_in,
        inv_vec,
        inv_smem,
        place_smem,
        source_smem,
        weights,
        kv_total,
        grads,
        lhs,
        ring_send,
        ring_recv,
        out_buf,
        in_sem,
        weight_sem,
        small_sem,
        a2a_send,
        a2a_recv,
        table_send,
        table_recv,
        ring_send_sem,
        ring_recv_sem,
        back_send,
        back_recv,
    ) = scratch[3 * count :]
    me = lax.axis_index("dp")
    z = lax.axis_index("mp")
    units, unit_rows, q_cols = q_hbm.shape
    kv_cols = k_hbm.shape[2]
    docs = units // DOC_UNITS
    core = lax.rem(me, CORES)
    x = lax.rem(me // CORES, GRID_X)
    y = me // (CORES * GRID_X)

    def peer(offset):
        dc = lax.rem(offset, CORES)
        dx = lax.rem(offset // CORES, GRID_X)
        dy = offset // (CORES * GRID_X)
        return (
            lax.rem(y + dy, GRID_Y) * GRID_X + lax.rem(x + dx, GRID_X)
        ) * CORES + lax.rem(core + dc, CORES)

    loads = []
    for p, heads in enumerate(phases):
        pieces = [] if p else [(k_hbm, 0, kv_cols), (v_hbm, 0, kv_cols)]
        for head in heads:
            pieces += [(q_hbm, head * HEAD, HEAD), (g_hbm, head * HEAD, HEAD)]
        at = 0
        for n, (ref, first, width) in enumerate(pieces):
            loads.append(
                (
                    p,
                    pltpu.make_async_copy(
                        ref.at[:, :, pl.ds(first, width)],
                        held[p].at[:, :, pl.ds(at, width)],
                        in_sem.at[len(loads)],
                    ),
                )
            )
            at += width
    for _, copy in loads:
        copy.start()
    weight_loads = [
        pltpu.make_async_copy(wq_hbm, weights.at[:, pl.ds(0, q_cols)], weight_sem.at[0]),
        pltpu.make_async_copy(wk_hbm, weights.at[:, pl.ds(q_cols, kv_cols)], weight_sem.at[1]),
        pltpu.make_async_copy(
            wv_hbm, weights.at[:, pl.ds(q_cols + kv_cols, kv_cols)], weight_sem.at[2]
        ),
    ]

    barrier = pltpu.get_barrier_semaphore()

    def greet(o, carry):
        pl.semaphore_signal(barrier, inc=1, device_id={"dp": peer(o)}, device_id_type=MESH)
        return carry

    lax.fori_loop(1, n_dp, greet, 0)
    right, left = lax.rem(z + 1, n_mp), lax.rem(z + n_mp - 1, n_mp)
    for near in (left, right):
        pl.semaphore_signal(barrier, inc=1, device_id={"mp": near}, device_id_type=MESH)

    lanes = lax.broadcasted_iota(jnp.int32, (8, 128), 1)
    unit_of = jnp.zeros((8, 128), jnp.int32)
    place_of = jnp.zeros((8, 128), jnp.int32)
    for u in range(units):
        hit = lanes == server_ref[u]
        unit_of = jnp.where(hit, u, unit_of)
        place_of = jnp.where(hit, place_ref[u], place_of)
    inv_vec[...] = unit_of
    table_out[...] = place_of[:1]
    table_in[me] = place_of[:1]
    to_smem = pltpu.make_async_copy(inv_vec, inv_smem, small_sem.at[0])
    to_smem.start()
    to_smem.wait()

    pl.semaphore_wait(barrier, n_dp - 1 + 2)

    def chip_peer(i, to_core):
        j = lax.rem(i * ORDER_STRIDE + ORDER_START, GRID_X * GRID_Y)
        dx = lax.rem(j, GRID_X)
        dy = j // GRID_X
        return (
            lax.rem(y + dy, GRID_Y) * GRID_X + lax.rem(x + dx, GRID_X)
        ) * CORES + to_core

    def send_table(o, carry):
        to = peer(o)
        pltpu.make_async_remote_copy(
            src_ref=table_out,
            dst_ref=table_in.at[me],
            send_sem=table_send.at[to],
            recv_sem=table_recv.at[me],
            device_id={"dp": to},
            device_id_type=MESH,
        ).start()
        return carry

    lax.fori_loop(1, n_dp, send_table, 0)

    for to_core in range(CORES):
        for p in range(count):
            if to_core == 0:
                for q, copy in loads:
                    if p == q:
                        copy.wait()
                recv[p][me] = held[p][inv_smem[0, me]]

            def send_unit(i, carry, p=p, to_core=to_core):
                to = chip_peer(i, to_core)

                @pl.when(to != me)
                def _():
                    stage[p][to] = held[p][inv_smem[0, to]]
                    pltpu.make_async_remote_copy(
                        src_ref=stage[p].at[to],
                        dst_ref=recv[p].at[me],
                        send_sem=a2a_send.at[p, to],
                        recv_sem=a2a_recv.at[p, me],
                        device_id={"dp": to},
                        device_id_type=MESH,
                    ).start()
                return carry

            lax.fori_loop(0, GRID_X * GRID_Y, send_unit, 0)
    for copy in weight_loads:
        copy.start()

    def table_arrived(o, carry):
        frm = peer(o)
        pltpu.make_async_remote_copy(
            src_ref=table_out,
            dst_ref=table_in.at[frm],
            send_sem=table_send.at[frm],
            recv_sem=table_recv.at[frm],
            device_id={"dp": frm},
            device_id_type=MESH,
        ).wait_recv()
        return carry

    lax.fori_loop(1, n_dp, table_arrived, 0)
    table = table_in[:, 0, :]
    wide = lax.broadcasted_iota(jnp.int32, (units, 128), 1)
    tall = lax.broadcasted_iota(jnp.int32, (units, 128), 0)
    place_col = jnp.sum(jnp.where(wide == me, table, 0), axis=1, keepdims=True)
    for n in range(units):
        place_smem[n] = jnp.max(jnp.where(tall == n, place_col, 0))
        source_smem[n] = jnp.max(jnp.where(place_col == n, tall, 0))

    block = DOC_UNITS * unit_rows
    score_scale = 1.0 / math.sqrt(HEAD)
    exponent_scale = score_scale * math.log2(math.e)

    def one_doc(p, doc):
        length = length_ref[doc]
        sources = [source_smem[doc * DOC_UNITS + i] for i in range(DOC_UNITS)]

        def rows(p, at):
            return jnp.concatenate(
                [recv[p][s, :, pl.ds(at, HEAD)] for s in sources], axis=0
            )

        key_at = lax.broadcasted_iota(jnp.int32, (block, block), 0)
        query_at = lax.broadcasted_iota(jnp.int32, (block, block), 1)
        allowed = (key_at <= query_at) & (key_at < length)
        live = lax.broadcasted_iota(jnp.int32, (block, HEAD), 0) < length
        keys, values = rows(0, 0), rows(0, kv_cols)
        if p == 0:
            key_grad = jnp.zeros((block, HEAD), jnp.float32)
            value_grad = jnp.zeros((block, HEAD), jnp.float32)
        else:
            key_grad, value_grad = kv_total[doc, 0], kv_total[doc, 1]

        def store(at, value):
            low = value.astype(jnp.bfloat16)
            for i in range(DOC_UNITS):
                grads[doc * DOC_UNITS + i, :, pl.ds(at, HEAD)] = low[
                    i * unit_rows : (i + 1) * unit_rows
                ]

        for n, head in enumerate(phases[p]):
            at = 2 * n * HEAD + (0 if p else 2 * kv_cols)
            queries = rows(p, at)
            masked = rows(p, at + HEAD)
            masked = jnp.where(live, masked, jnp.zeros_like(masked))
            scores = jnp.where(allowed, dot(keys, queries, NT), -1e30)
            peak = jnp.max(scores, axis=0, keepdims=True)
            expanded = jnp.exp2((scores - peak) * exponent_scale)
            probs = expanded * (1.0 / jnp.sum(expanded, axis=0, keepdims=True))
            probs_low = probs.astype(jnp.bfloat16)
            prob_grad = dot(values, masked, NT)
            delta = jnp.sum(probs_low.astype(jnp.float32) * prob_grad, axis=0, keepdims=True)
            score_low = (probs * (prob_grad - delta)).astype(jnp.bfloat16)
            value_grad += dot(probs_low, masked, NN)
            key_grad += dot(score_low, queries, NN)
            store(head * HEAD, dot(score_low, keys, TN) * score_scale)
        if p == count - 1:
            store(q_cols, key_grad * score_scale)
            store(q_cols + kv_cols, value_grad)
        else:
            kv_total[doc, 0] = key_grad
            kv_total[doc, 1] = value_grad

    def unit_copy(p, frm):
        return pltpu.make_async_remote_copy(
            src_ref=stage[p].at[frm],
            dst_ref=recv[p].at[frm],
            send_sem=a2a_send.at[p, frm],
            recv_sem=a2a_recv.at[p, frm],
            device_id={"dp": frm},
            device_id_type=MESH,
        )

    for p in range(count):

        def unit_arrived(o, carry, p=p):
            unit_copy(p, peer(o)).wait_recv()
            return carry

        lax.fori_loop(1, n_dp, unit_arrived, 0)

        def doc_phase(doc, carry, p=p):
            one_doc(p, doc)
            return carry

        lax.fori_loop(0, docs, doc_phase, 0)
    for copy in weight_loads:
        copy.wait()

    chunks = units // CHUNK_UNITS
    chunk_rows = CHUNK_UNITS * unit_rows
    half = chunk_rows // 2
    out_cols = out_hbm.shape[2]
    far = n_mp // 2

    def part(chunk, distance):
        column = lax.rem(z + distance, n_mp) * out_cols
        return dot(
            lhs[chunk],
            weights[pl.ds(pl.multiple_of(column, out_cols), out_cols), :],
            NT,
        )

    def ring_copy(chunk, way, step):
        first, count = (0, chunk_rows) if step else (way * half, half)
        return pltpu.make_async_remote_copy(
            src_ref=ring_send.at[chunk, way, step, pl.ds(first, count), :],
            dst_ref=ring_recv.at[chunk, way, step, pl.ds(first, count), :],
            send_sem=ring_send_sem.at[chunk, way, step],
            recv_sem=ring_recv_sem.at[chunk, way, step],
            device_id={"mp": left if way else right},
            device_id_type=MESH,
        )

    def back_copy(o):
        to = peer(n_dp - 1 - o)
        return pltpu.make_async_remote_copy(
            src_ref=out_buf.at[o],
            dst_ref=out_hbm.at[me],
            send_sem=back_send.at[to],
            recv_sem=back_recv.at[me],
            device_id={"dp": to},
            device_id_type=MESH,
        )

    def first_step(chunk, carry):
        for i in range(CHUNK_UNITS):
            s = peer(n_dp - 1 - (chunk * CHUNK_UNITS + i))
            lhs[chunk, pl.ds(i * unit_rows, unit_rows), :] = grads[place_smem[s]]
        low = part(chunk, far).astype(jnp.bfloat16)
        for way in range(2):
            ring_send[chunk, way, 0, pl.ds(way * half, half), :] = low[
                way * half : (way + 1) * half
            ]
            ring_copy(chunk, way, 0).start()
        return carry

    lax.fori_loop(0, chunks, first_step, 0)

    for step in range(1, far):

        def next_step(chunk, carry, step=step):
            for way in range(2):
                total = part(chunk, n_mp - far + step if way else far - step)
                ring_copy(chunk, way, step - 1).wait_recv()
                for h in range(2):
                    piece = total[h * half : (h + 1) * half]
                    if step > 1 or h == way:
                        piece += ring_recv[
                            chunk, way, step - 1, pl.ds(h * half, half), :
                        ].astype(jnp.float32)
                    ring_send[chunk, way, step, pl.ds(h * half, half), :] = piece.astype(
                        jnp.bfloat16
                    )
                ring_copy(chunk, way, step).start()
            return carry

        lax.fori_loop(0, chunks, next_step, 0)

    own_copy = pltpu.make_async_copy(out_buf.at[n_dp - 1], out_hbm.at[me], small_sem.at[2])

    def last_step(chunk, carry):
        total = part(chunk, 0)
        for way in range(2):
            ring_copy(chunk, way, far - 1).wait_recv()
            total += ring_recv[chunk, way, far - 1].astype(jnp.float32)
        low = total.astype(jnp.bfloat16)
        for i in range(CHUNK_UNITS):
            out_buf[chunk * CHUNK_UNITS + i] = low[i * unit_rows : (i + 1) * unit_rows]
        for i in range(CHUNK_UNITS - 1):
            back_copy(chunk * CHUNK_UNITS + i).start()

        @pl.when(chunk < chunks - 1)
        def _():
            back_copy(chunk * CHUNK_UNITS + CHUNK_UNITS - 1).start()

        @pl.when(chunk == chunks - 1)
        def _():
            own_copy.start()

        return carry

    lax.fori_loop(0, chunks, last_step, 0)
    own_copy.wait()

    def exchange_done(o, carry):
        to = peer(o)
        pltpu.make_async_remote_copy(
            src_ref=table_out,
            dst_ref=table_in.at[to],
            send_sem=table_send.at[to],
            recv_sem=table_recv.at[to],
            device_id={"dp": to},
            device_id_type=MESH,
        ).wait_send()
        for p in range(count):
            unit_copy(p, to).wait_send()
        return carry

    lax.fori_loop(1, n_dp, exchange_done, 0)

    def ring_done(chunk, carry):
        for way in range(2):
            for step in range(far):
                ring_copy(chunk, way, step).wait_send()
        return carry

    lax.fori_loop(0, chunks, ring_done, 0)

    def back_arrived(o, carry):
        frm = peer(o)
        pltpu.make_async_remote_copy(
            src_ref=out_buf.at[o],
            dst_ref=out_hbm.at[frm],
            send_sem=back_send.at[frm],
            recv_sem=back_recv.at[frm],
            device_id={"dp": frm},
            device_id_type=MESH,
        ).wait()
        return carry

    lax.fori_loop(1, n_dp, back_arrived, 0)


def settle(server_ref, back_hbm, out_hbm, held, wide, in_sem, out_sem):
    units, unit_rows = held.shape[:2]
    rows = units * unit_rows // SETTLE_STEPS

    def fetch(u):
        return pltpu.make_async_copy(back_hbm.at[server_ref[u]], held.at[u], in_sem.at[u])

    def emit(step):
        part = pl.ds(step * rows, rows)
        return pltpu.make_async_copy(wide.at[part, :], out_hbm.at[part, :], out_sem.at[step])

    for u in range(units):
        fetch(u).start()
    for step in range(SETTLE_STEPS):
        for u in range(step * units // SETTLE_STEPS, (step + 1) * units // SETTLE_STEPS):
            fetch(u).wait()
            wide[pl.ds(u * unit_rows, unit_rows), :] = held[u].astype(jnp.float32)
        emit(step).start()
    for step in range(SETTLE_STEPS):
        emit(step).wait()


def local(
    saved_query,
    saved_key,
    saved_value,
    grad_output,
    unit_server,
    unit_place,
    doc_length,
    query_weight,
    key_weight,
    value_weight,
):
    n_dp, n_mp = lax.axis_size("dp"), lax.axis_size("mp")
    units = unit_server.shape[0]
    unit_rows = saved_query.shape[0] // units
    q_cols, kv_cols = saved_query.shape[1], saved_key.shape[1]
    out_all = query_weight.shape[0]
    out_cols = out_all // n_mp
    k_cols = q_cols + 2 * kv_cols
    heads = q_cols // HEAD
    phases = [range(0, 1), range(1, heads - 1), range(heads - 1, heads)]
    widths = [2 * HEAD * len(p) for p in phases]
    widths[0] += 2 * kv_cols
    chunks = units // CHUNK_UNITS
    chunk_rows = CHUNK_UNITS * unit_rows
    far = n_mp // 2
    low = jnp.bfloat16

    def split(a):
        return a.reshape(units, unit_rows, a.shape[1])

    smem = pl.BlockSpec(memory_space=pltpu.SMEM)
    hbm = pl.BlockSpec(memory_space=pl.ANY)
    dma = pltpu.SemaphoreType.DMA
    back = pl.pallas_call(
        functools.partial(kernel, n_dp, n_mp, phases),
        out_shape=jax.ShapeDtypeStruct((n_dp, unit_rows, out_cols), low),
        in_specs=[smem] * 3 + [hbm] * 7,
        out_specs=hbm,
        scratch_shapes=[
            *[pltpu.VMEM((units, unit_rows, w), low) for w in widths],
            *[pltpu.VMEM((n_dp, unit_rows, w), low) for w in widths],
            *[pltpu.VMEM((n_dp, unit_rows, w), low) for w in widths],
            pltpu.VMEM((1, 128), jnp.int32),
            pltpu.VMEM((n_dp, 1, 128), jnp.int32),
            pltpu.VMEM((8, 128), jnp.int32),
            pltpu.SMEM((8, 128), jnp.int32),
            pltpu.SMEM((units,), jnp.int32),
            pltpu.SMEM((units,), jnp.int32),
            pltpu.VMEM((out_all, k_cols), low),
            pltpu.VMEM((units // DOC_UNITS, 2, DOC_UNITS * unit_rows, HEAD), jnp.float32),
            pltpu.VMEM((units, unit_rows, k_cols), low),
            pltpu.VMEM((chunks, chunk_rows, k_cols), low),
            pltpu.VMEM((chunks, 2, far, chunk_rows, out_cols), low),
            pltpu.VMEM((chunks, 2, far, chunk_rows, out_cols), low),
            pltpu.VMEM((units, unit_rows, out_cols), low),
            dma((2 + 2 * heads,)),
            dma((3,)),
            dma((3,)),
            dma((len(phases), n_dp)),
            dma((len(phases), n_dp)),
            dma((n_dp,)),
            dma((n_dp,)),
            dma((chunks, 2, far)),
            dma((chunks, 2, far)),
            dma((n_dp,)),
            dma((n_dp,)),
        ],
        compiler_params=pltpu.CompilerParams(
            collective_id=0, has_side_effects=True, vmem_limit_bytes=60 * 1024 * 1024
        ),
        name="attention_backward_exchange",
    )(
        unit_server,
        unit_place,
        doc_length,
        split(saved_query),
        split(saved_key),
        split(saved_value),
        split(grad_output),
        query_weight,
        key_weight,
        value_weight,
    )
    return pl.pallas_call(
        settle,
        out_shape=jax.ShapeDtypeStruct((units * unit_rows, out_cols), jnp.float32),
        in_specs=[smem, hbm],
        out_specs=hbm,
        scratch_shapes=[
            pltpu.VMEM((units, unit_rows, out_cols), low),
            pltpu.VMEM((units * unit_rows, out_cols), jnp.float32),
            dma((units,)),
            dma((SETTLE_STEPS,)),
        ],
        name="settle_rows",
    )(unit_server, back)


def solution(mesh):
    placed = (
        P("dp", "mp"),
        P("dp", "mp"),
        P("dp", "mp"),
        P("dp", "mp"),
        P("dp"),
        P("dp"),
        P("dp"),
        P(None, "mp"),
        P(None, "mp"),
        P(None, "mp"),
    )
    return jax.shard_map(
        local, mesh=mesh, in_specs=placed, out_specs=P("dp", "mp"), check_vma=False
    )
```

```python
import functools
import math

import jax
import jax.numpy as jnp
from jax import lax
from jax.experimental import pallas as pl
from jax.experimental.pallas import tpu as pltpu
from jax.sharding import PartitionSpec as P

HEAD = 128
DOC_UNITS = 8
MESH = pl.DeviceIdType.MESH
NT = (((1,), (1,)), ((), ()))
NN = (((1,), (0,)), ((), ()))
TN = (((0,), (0,)), ((), ()))
CHUNK_UNITS = 4
SETTLE_STEPS = 8
GRID_Y, GRID_X, CORES = 4, 4, 2
ORDER_STRIDE, ORDER_START = 11, 3


def dot(a, b, numbers):
    return lax.dot_general(a, b, numbers, preferred_element_type=jnp.float32)


def kernel(
    n_dp,
    n_mp,
    phases,
    server_ref,
    place_ref,
    length_ref,
    q_hbm,
    k_hbm,
    v_hbm,
    g_hbm,
    wq_hbm,
    wk_hbm,
    wv_hbm,
    out_hbm,
    *scratch,
):
    count = len(phases)
    held, stage, recv = scratch[:count], scratch[count : 2 * count], scratch[2 * count : 3 * count]
    (
        table_out,
        table_in,
        inv_vec,
        inv_smem,
        place_smem,
        source_smem,
        weights,
        kv_total,
        grads,
        lhs,
        ring_send,
        ring_recv,
        out_buf,
        in_sem,
        weight_sem,
        small_sem,
        a2a_send,
        a2a_recv,
        table_send,
        table_recv,
        ring_send_sem,
        ring_recv_sem,
        back_send,
        back_recv,
    ) = scratch[3 * count :]
    me = lax.axis_index("dp")
    z = lax.axis_index("mp")
    units, unit_rows, q_cols = q_hbm.shape
    kv_cols = k_hbm.shape[2]
    docs = units // DOC_UNITS
    core = lax.rem(me, CORES)
    x = lax.rem(me // CORES, GRID_X)
    y = me // (CORES * GRID_X)

    def peer(offset):
        dc = lax.rem(offset, CORES)
        dx = lax.rem(offset // CORES, GRID_X)
        dy = offset // (CORES * GRID_X)
        return (
            lax.rem(y + dy, GRID_Y) * GRID_X + lax.rem(x + dx, GRID_X)
        ) * CORES + lax.rem(core + dc, CORES)

    loads = []
    for p, heads in enumerate(phases):
        pieces = [] if p else [(k_hbm, 0, kv_cols), (v_hbm, 0, kv_cols)]
        for head in heads:
            pieces += [(q_hbm, head * HEAD, HEAD), (g_hbm, head * HEAD, HEAD)]
        at = 0
        for n, (ref, first, width) in enumerate(pieces):
            loads.append(
                (
                    p,
                    pltpu.make_async_copy(
                        ref.at[:, :, pl.ds(first, width)],
                        held[p].at[:, :, pl.ds(at, width)],
                        in_sem.at[len(loads)],
                    ),
                )
            )
            at += width
    for _, copy in loads:
        copy.start()
    weight_loads = [
        pltpu.make_async_copy(wq_hbm, weights.at[:, pl.ds(0, q_cols)], weight_sem.at[0]),
        pltpu.make_async_copy(wk_hbm, weights.at[:, pl.ds(q_cols, kv_cols)], weight_sem.at[1]),
        pltpu.make_async_copy(
            wv_hbm, weights.at[:, pl.ds(q_cols + kv_cols, kv_cols)], weight_sem.at[2]
        ),
    ]

    barrier = pltpu.get_barrier_semaphore()

    def greet(o, carry):
        pl.semaphore_signal(barrier, inc=1, device_id={"dp": peer(o)}, device_id_type=MESH)
        return carry

    lax.fori_loop(1, n_dp, greet, 0)
    right, left = lax.rem(z + 1, n_mp), lax.rem(z + n_mp - 1, n_mp)
    for near in (left, right):
        pl.semaphore_signal(barrier, inc=1, device_id={"mp": near}, device_id_type=MESH)

    lanes = lax.broadcasted_iota(jnp.int32, (8, 128), 1)
    unit_of = jnp.zeros((8, 128), jnp.int32)
    place_of = jnp.zeros((8, 128), jnp.int32)
    for u in range(units):
        hit = lanes == server_ref[u]
        unit_of = jnp.where(hit, u, unit_of)
        place_of = jnp.where(hit, place_ref[u], place_of)
    inv_vec[...] = unit_of
    table_out[...] = place_of[:1]
    table_in[me] = place_of[:1]
    to_smem = pltpu.make_async_copy(inv_vec, inv_smem, small_sem.at[0])
    to_smem.start()
    to_smem.wait()

    pl.semaphore_wait(barrier, n_dp - 1 + 2)

    def chip_peer(i, to_core):
        j = lax.rem(i * ORDER_STRIDE + ORDER_START, GRID_X * GRID_Y)
        dx = lax.rem(j, GRID_X)
        dy = j // GRID_X
        return (
            lax.rem(y + dy, GRID_Y) * GRID_X + lax.rem(x + dx, GRID_X)
        ) * CORES + to_core

    def send_table(o, carry):
        to = peer(o)
        pltpu.make_async_remote_copy(
            src_ref=table_out,
            dst_ref=table_in.at[me],
            send_sem=table_send.at[to],
            recv_sem=table_recv.at[me],
            device_id={"dp": to},
            device_id_type=MESH,
        ).start()
        return carry

    lax.fori_loop(1, n_dp, send_table, 0)

    for to_core in range(CORES):
        for p in range(count):
            if to_core == 0:
                for q, copy in loads:
                    if p == q:
                        copy.wait()
                recv[p][me] = held[p][inv_smem[0, me]]

            def send_unit(i, carry, p=p, to_core=to_core):
                to = chip_peer(i, to_core)

                @pl.when(to != me)
                def _():
                    stage[p][to] = held[p][inv_smem[0, to]]
                    pltpu.make_async_remote_copy(
                        src_ref=stage[p].at[to],
                        dst_ref=recv[p].at[me],
                        send_sem=a2a_send.at[p, to],
                        recv_sem=a2a_recv.at[p, me],
                        device_id={"dp": to},
                        device_id_type=MESH,
                    ).start()
                return carry

            lax.fori_loop(0, GRID_X * GRID_Y, send_unit, 0)
    for copy in weight_loads:
        copy.start()

    def table_arrived(o, carry):
        frm = peer(o)
        pltpu.make_async_remote_copy(
            src_ref=table_out,
            dst_ref=table_in.at[frm],
            send_sem=table_send.at[frm],
            recv_sem=table_recv.at[frm],
            device_id={"dp": frm},
            device_id_type=MESH,
        ).wait_recv()
        return carry

    lax.fori_loop(1, n_dp, table_arrived, 0)
    table = table_in[:, 0, :]
    wide = lax.broadcasted_iota(jnp.int32, (units, 128), 1)
    tall = lax.broadcasted_iota(jnp.int32, (units, 128), 0)
    place_col = jnp.sum(jnp.where(wide == me, table, 0), axis=1, keepdims=True)
    for n in range(units):
        place_smem[n] = jnp.max(jnp.where(tall == n, place_col, 0))
        source_smem[n] = jnp.max(jnp.where(place_col == n, tall, 0))

    block = DOC_UNITS * unit_rows
    score_scale = 1.0 / math.sqrt(HEAD)
    exponent_scale = score_scale * math.log2(math.e)

    def one_doc(p, doc):
        length = length_ref[doc]
        sources = [source_smem[doc * DOC_UNITS + i] for i in range(DOC_UNITS)]

        def rows(p, at):
            return jnp.concatenate(
                [recv[p][s, :, pl.ds(at, HEAD)] for s in sources], axis=0
            )

        key_at = lax.broadcasted_iota(jnp.int32, (block, block), 0)
        query_at = lax.broadcasted_iota(jnp.int32, (block, block), 1)
        allowed = (key_at <= query_at) & (key_at < length)
        live = lax.broadcasted_iota(jnp.int32, (block, HEAD), 0) < length
        keys, values = rows(0, 0), rows(0, kv_cols)
        if p == 0:
            key_grad = jnp.zeros((block, HEAD), jnp.float32)
            value_grad = jnp.zeros((block, HEAD), jnp.float32)
        else:
            key_grad, value_grad = kv_total[doc, 0], kv_total[doc, 1]

        def store(at, value):
            low = value.astype(jnp.bfloat16)
            for i in range(DOC_UNITS):
                grads[doc * DOC_UNITS + i, :, pl.ds(at, HEAD)] = low[
                    i * unit_rows : (i + 1) * unit_rows
                ]

        for n, head in enumerate(phases[p]):
            at = 2 * n * HEAD + (0 if p else 2 * kv_cols)
            queries = rows(p, at)
            masked = rows(p, at + HEAD)
            masked = jnp.where(live, masked, jnp.zeros_like(masked))
            scores = jnp.where(allowed, dot(keys, queries, NT), -1e30)
            peak = jnp.max(scores, axis=0, keepdims=True)
            expanded = jnp.exp2((scores - peak) * exponent_scale)
            probs = expanded * (1.0 / jnp.sum(expanded, axis=0, keepdims=True))
            probs_low = probs.astype(jnp.bfloat16)
            prob_grad = dot(values, masked, NT)
            delta = jnp.sum(probs_low.astype(jnp.float32) * prob_grad, axis=0, keepdims=True)
            score_low = (probs * (prob_grad - delta)).astype(jnp.bfloat16)
            value_grad += dot(probs_low, masked, NN)
            key_grad += dot(score_low, queries, NN)
            store(head * HEAD, dot(score_low, keys, TN) * score_scale)
        if p == count - 1:
            store(q_cols, key_grad * score_scale)
            store(q_cols + kv_cols, value_grad)
        else:
            kv_total[doc, 0] = key_grad
            kv_total[doc, 1] = value_grad

    def unit_copy(p, frm):
        return pltpu.make_async_remote_copy(
            src_ref=stage[p].at[frm],
            dst_ref=recv[p].at[frm],
            send_sem=a2a_send.at[p, frm],
            recv_sem=a2a_recv.at[p, frm],
            device_id={"dp": frm},
            device_id_type=MESH,
        )

    for p in range(count):

        def unit_arrived(o, carry, p=p):
            unit_copy(p, peer(o)).wait_recv()
            return carry

        lax.fori_loop(1, n_dp, unit_arrived, 0)

        def doc_phase(doc, carry, p=p):
            one_doc(p, doc)
            return carry

        lax.fori_loop(0, docs, doc_phase, 0)
    for copy in weight_loads:
        copy.wait()

    chunks = units // CHUNK_UNITS
    chunk_rows = CHUNK_UNITS * unit_rows
    half = chunk_rows // 2
    out_cols = out_hbm.shape[2]
    far = n_mp // 2

    def part(chunk, distance):
        column = lax.rem(z + distance, n_mp) * out_cols
        return dot(
            lhs[chunk],
            weights[pl.ds(pl.multiple_of(column, out_cols), out_cols), :],
            NT,
        )

    def ring_copy(chunk, way, step):
        first, count = (0, chunk_rows) if step else (way * half, half)
        return pltpu.make_async_remote_copy(
            src_ref=ring_send.at[chunk, way, step, pl.ds(first, count), :],
            dst_ref=ring_recv.at[chunk, way, step, pl.ds(first, count), :],
            send_sem=ring_send_sem.at[chunk, way, step],
            recv_sem=ring_recv_sem.at[chunk, way, step],
            device_id={"mp": left if way else right},
            device_id_type=MESH,
        )

    def back_copy(o):
        to = peer(n_dp - 1 - o)
        return pltpu.make_async_remote_copy(
            src_ref=out_buf.at[o],
            dst_ref=out_hbm.at[me],
            send_sem=back_send.at[to],
            recv_sem=back_recv.at[me],
            device_id={"dp": to},
            device_id_type=MESH,
        )

    def first_step(chunk, carry):
        for i in range(CHUNK_UNITS):
            s = peer(n_dp - 1 - (chunk * CHUNK_UNITS + i))
            lhs[chunk, pl.ds(i * unit_rows, unit_rows), :] = grads[place_smem[s]]
        low = part(chunk, far).astype(jnp.bfloat16)
        for way in range(2):
            ring_send[chunk, way, 0, pl.ds(way * half, half), :] = low[
                way * half : (way + 1) * half
            ]
            ring_copy(chunk, way, 0).start()
        return carry

    lax.fori_loop(0, chunks, first_step, 0)

    for step in range(1, far):

        def next_step(chunk, carry, step=step):
            for way in range(2):
                total = part(chunk, n_mp - far + step if way else far - step)
                ring_copy(chunk, way, step - 1).wait_recv()
                for h in range(2):
                    piece = total[h * half : (h + 1) * half]
                    if step > 1 or h == way:
                        piece += ring_recv[
                            chunk, way, step - 1, pl.ds(h * half, half), :
                        ].astype(jnp.float32)
                    ring_send[chunk, way, step, pl.ds(h * half, half), :] = piece.astype(
                        jnp.bfloat16
                    )
                ring_copy(chunk, way, step).start()
            return carry

        lax.fori_loop(0, chunks, next_step, 0)

    own_copy = pltpu.make_async_copy(out_buf.at[n_dp - 1], out_hbm.at[me], small_sem.at[2])

    def last_step(chunk, carry):
        total = part(chunk, 0)
        for way in range(2):
            ring_copy(chunk, way, far - 1).wait_recv()
            total += ring_recv[chunk, way, far - 1].astype(jnp.float32)
        low = total.astype(jnp.bfloat16)
        for i in range(CHUNK_UNITS):
            out_buf[chunk * CHUNK_UNITS + i] = low[i * unit_rows : (i + 1) * unit_rows]
        for i in range(CHUNK_UNITS - 1):
            back_copy(chunk * CHUNK_UNITS + i).start()

        @pl.when(chunk < chunks - 1)
        def _():
            back_copy(chunk * CHUNK_UNITS + CHUNK_UNITS - 1).start()

        @pl.when(chunk == chunks - 1)
        def _():
            own_copy.start()

        return carry

    lax.fori_loop(0, chunks, last_step, 0)
    own_copy.wait()

    def exchange_done(o, carry):
        to = peer(o)
        pltpu.make_async_remote_copy(
            src_ref=table_out,
            dst_ref=table_in.at[to],
            send_sem=table_send.at[to],
            recv_sem=table_recv.at[to],
            device_id={"dp": to},
            device_id_type=MESH,
        ).wait_send()
        for p in range(count):
            unit_copy(p, to).wait_send()
        return carry

    lax.fori_loop(1, n_dp, exchange_done, 0)

    def ring_done(chunk, carry):
        for way in range(2):
            for step in range(far):
                ring_copy(chunk, way, step).wait_send()
        return carry

    lax.fori_loop(0, chunks, ring_done, 0)

    def back_arrived(o, carry):
        frm = peer(o)
        pltpu.make_async_remote_copy(
            src_ref=out_buf.at[o],
            dst_ref=out_hbm.at[frm],
            send_sem=back_send.at[frm],
            recv_sem=back_recv.at[frm],
            device_id={"dp": frm},
            device_id_type=MESH,
        ).wait()
        return carry

    lax.fori_loop(1, n_dp, back_arrived, 0)


def settle(server_hbm, back_hbm, out_hbm, server, held, wide, server_sem, in_sem, out_sem):
    units, unit_rows = held.shape[:2]
    rows = units * unit_rows // SETTLE_STEPS
    share = units // SETTLE_STEPS
    table = pltpu.make_async_copy(server_hbm, server, server_sem)

    def fetch(step):
        part = pl.ds(step * share, share)
        return pltpu.make_async_copy(back_hbm.at[part], held.at[part], in_sem.at[step])

    def emit(step):
        part = pl.ds(step * rows, rows)
        return pltpu.make_async_copy(wide.at[part, :], out_hbm.at[part, :], out_sem.at[step])

    table.start()
    for step in range(SETTLE_STEPS):
        fetch(step).start()
    table.wait()
    for step in range(SETTLE_STEPS):
        fetch(step).wait()
    for step in range(SETTLE_STEPS):
        for u in range(step * share, (step + 1) * share):
            wide[pl.ds(u * unit_rows, unit_rows), :] = held[server[u]].astype(jnp.float32)
        emit(step).start()
    for step in range(SETTLE_STEPS):
        emit(step).wait()


def local(
    saved_query,
    saved_key,
    saved_value,
    grad_output,
    unit_server,
    unit_place,
    doc_length,
    query_weight,
    key_weight,
    value_weight,
):
    n_dp, n_mp = lax.axis_size("dp"), lax.axis_size("mp")
    units = unit_server.shape[0]
    unit_rows = saved_query.shape[0] // units
    q_cols, kv_cols = saved_query.shape[1], saved_key.shape[1]
    out_all = query_weight.shape[0]
    out_cols = out_all // n_mp
    k_cols = q_cols + 2 * kv_cols
    heads = q_cols // HEAD
    phases = [range(h, h + 1) for h in range(heads)]
    widths = [2 * HEAD * len(p) for p in phases]
    widths[0] += 2 * kv_cols
    chunks = units // CHUNK_UNITS
    chunk_rows = CHUNK_UNITS * unit_rows
    far = n_mp // 2
    low = jnp.bfloat16

    def split(a):
        return a.reshape(units, unit_rows, a.shape[1])

    smem = pl.BlockSpec(memory_space=pltpu.SMEM)
    hbm = pl.BlockSpec(memory_space=pl.ANY)
    dma = pltpu.SemaphoreType.DMA
    back = pl.pallas_call(
        functools.partial(kernel, n_dp, n_mp, phases),
        out_shape=jax.ShapeDtypeStruct((n_dp, unit_rows, out_cols), low),
        in_specs=[smem] * 3 + [hbm] * 7,
        out_specs=hbm,
        scratch_shapes=[
            *[pltpu.VMEM((units, unit_rows, w), low) for w in widths],
            *[pltpu.VMEM((n_dp, unit_rows, w), low) for w in widths],
            *[pltpu.VMEM((n_dp, unit_rows, w), low) for w in widths],
            pltpu.VMEM((1, 128), jnp.int32),
            pltpu.VMEM((n_dp, 1, 128), jnp.int32),
            pltpu.VMEM((8, 128), jnp.int32),
            pltpu.SMEM((8, 128), jnp.int32),
            pltpu.SMEM((units,), jnp.int32),
            pltpu.SMEM((units,), jnp.int32),
            pltpu.VMEM((out_all, k_cols), low),
            pltpu.VMEM((units // DOC_UNITS, 2, DOC_UNITS * unit_rows, HEAD), jnp.float32),
            pltpu.VMEM((units, unit_rows, k_cols), low),
            pltpu.VMEM((chunks, chunk_rows, k_cols), low),
            pltpu.VMEM((chunks, 2, far, chunk_rows, out_cols), low),
            pltpu.VMEM((chunks, 2, far, chunk_rows, out_cols), low),
            pltpu.VMEM((units, unit_rows, out_cols), low),
            dma((2 + 2 * heads,)),
            dma((3,)),
            dma((3,)),
            dma((len(phases), n_dp)),
            dma((len(phases), n_dp)),
            dma((n_dp,)),
            dma((n_dp,)),
            dma((chunks, 2, far)),
            dma((chunks, 2, far)),
            dma((n_dp,)),
            dma((n_dp,)),
        ],
        compiler_params=pltpu.CompilerParams(
            collective_id=0, has_side_effects=True, vmem_limit_bytes=60 * 1024 * 1024
        ),
        name="attention_backward_exchange",
    )(
        unit_server,
        unit_place,
        doc_length,
        split(saved_query),
        split(saved_key),
        split(saved_value),
        split(grad_output),
        query_weight,
        key_weight,
        value_weight,
    )
    return pl.pallas_call(
        settle,
        out_shape=jax.ShapeDtypeStruct((units * unit_rows, out_cols), jnp.float32),
        in_specs=[hbm, hbm],
        out_specs=hbm,
        scratch_shapes=[
            pltpu.SMEM((units,), jnp.int32),
            pltpu.VMEM((units, unit_rows, out_cols), low),
            pltpu.VMEM((units * unit_rows, out_cols), jnp.float32),
            dma,
            dma((SETTLE_STEPS,)),
            dma((SETTLE_STEPS,)),
        ],
        name="settle_rows",
    )(unit_server, back)


def solution(mesh):
    placed = (
        P("dp", "mp"),
        P("dp", "mp"),
        P("dp", "mp"),
        P("dp", "mp"),
        P("dp"),
        P("dp"),
        P("dp"),
        P(None, "mp"),
        P(None, "mp"),
        P(None, "mp"),
    )
    return jax.shard_map(
        local, mesh=mesh, in_specs=placed, out_specs=P("dp", "mp"), check_vma=False
    )
```

```python
import functools
import math

import jax
import jax.numpy as jnp
from jax import lax
from jax.experimental import pallas as pl
from jax.experimental.pallas import tpu as pltpu
from jax.sharding import PartitionSpec as P

HEAD = 128
DOC_UNITS = 8
MESH = pl.DeviceIdType.MESH
NT = (((1,), (1,)), ((), ()))
NN = (((1,), (0,)), ((), ()))
TN = (((0,), (0,)), ((), ()))
CHUNK_UNITS = 4
SETTLE_STEPS = 8
GRID_Y, GRID_X, CORES = 4, 4, 2
ORDER_STRIDE, ORDER_START = 11, 3


def dot(a, b, numbers):
    return lax.dot_general(a, b, numbers, preferred_element_type=jnp.float32)


def kernel(
    n_dp,
    n_mp,
    phases,
    server_ref,
    place_ref,
    length_ref,
    q_hbm,
    k_hbm,
    v_hbm,
    g_hbm,
    wq_hbm,
    wk_hbm,
    wv_hbm,
    out_hbm,
    *scratch,
):
    count = len(phases)
    held, stage, recv = scratch[:count], scratch[count : 2 * count], scratch[2 * count : 3 * count]
    (
        table_out,
        table_in,
        inv_vec,
        inv_smem,
        place_smem,
        source_smem,
        weights,
        kv_total,
        grads,
        lhs,
        ring_send,
        ring_recv,
        out_buf,
        in_sem,
        weight_sem,
        small_sem,
        a2a_send,
        a2a_recv,
        table_send,
        table_recv,
        ring_send_sem,
        ring_recv_sem,
        back_send,
        back_recv,
    ) = scratch[3 * count :]
    me = lax.axis_index("dp")
    z = lax.axis_index("mp")
    units, unit_rows, q_cols = q_hbm.shape
    kv_cols = k_hbm.shape[2]
    docs = units // DOC_UNITS
    core = lax.rem(me, CORES)
    x = lax.rem(me // CORES, GRID_X)
    y = me // (CORES * GRID_X)

    def peer(offset):
        dc = lax.rem(offset, CORES)
        dx = lax.rem(offset // CORES, GRID_X)
        dy = offset // (CORES * GRID_X)
        return (
            lax.rem(y + dy, GRID_Y) * GRID_X + lax.rem(x + dx, GRID_X)
        ) * CORES + lax.rem(core + dc, CORES)

    loads = []
    for p, heads in enumerate(phases):
        pieces = [] if p else [(k_hbm, 0, kv_cols), (v_hbm, 0, kv_cols)]
        for head in heads:
            pieces += [(q_hbm, head * HEAD, HEAD), (g_hbm, head * HEAD, HEAD)]
        at = 0
        for n, (ref, first, width) in enumerate(pieces):
            loads.append(
                (
                    p,
                    pltpu.make_async_copy(
                        ref.at[:, :, pl.ds(first, width)],
                        held[p].at[:, :, pl.ds(at, width)],
                        in_sem.at[len(loads)],
                    ),
                )
            )
            at += width
    for _, copy in loads:
        copy.start()
    weight_loads = [
        pltpu.make_async_copy(wq_hbm, weights.at[:, pl.ds(0, q_cols)], weight_sem.at[0]),
        pltpu.make_async_copy(wk_hbm, weights.at[:, pl.ds(q_cols, kv_cols)], weight_sem.at[1]),
        pltpu.make_async_copy(
            wv_hbm, weights.at[:, pl.ds(q_cols + kv_cols, kv_cols)], weight_sem.at[2]
        ),
    ]

    barrier = pltpu.get_barrier_semaphore()

    def greet(o, carry):
        pl.semaphore_signal(barrier, inc=1, device_id={"dp": peer(o)}, device_id_type=MESH)
        return carry

    lax.fori_loop(1, n_dp, greet, 0)
    right, left = lax.rem(z + 1, n_mp), lax.rem(z + n_mp - 1, n_mp)
    for near in (left, right):
        pl.semaphore_signal(barrier, inc=1, device_id={"mp": near}, device_id_type=MESH)

    lanes = lax.broadcasted_iota(jnp.int32, (8, 128), 1)
    unit_of = jnp.zeros((8, 128), jnp.int32)
    place_of = jnp.zeros((8, 128), jnp.int32)
    for u in range(units):
        hit = lanes == server_ref[u]
        unit_of = jnp.where(hit, u, unit_of)
        place_of = jnp.where(hit, place_ref[u], place_of)
    inv_vec[...] = unit_of
    table_out[...] = place_of[:1]
    table_in[me] = place_of[:1]
    to_smem = pltpu.make_async_copy(inv_vec, inv_smem, small_sem.at[0])
    to_smem.start()
    to_smem.wait()

    pl.semaphore_wait(barrier, n_dp - 1 + 2)

    def chip_peer(i, to_core):
        j = lax.rem(i * ORDER_STRIDE + ORDER_START, GRID_X * GRID_Y)
        dx = lax.rem(j, GRID_X)
        dy = j // GRID_X
        return (
            lax.rem(y + dy, GRID_Y) * GRID_X + lax.rem(x + dx, GRID_X)
        ) * CORES + to_core

    def send_table(o, carry):
        to = peer(o)
        pltpu.make_async_remote_copy(
            src_ref=table_out,
            dst_ref=table_in.at[me],
            send_sem=table_send.at[to],
            recv_sem=table_recv.at[me],
            device_id={"dp": to},
            device_id_type=MESH,
        ).start()
        return carry

    lax.fori_loop(1, n_dp, send_table, 0)

    def unit_copy(p, frm):
        return pltpu.make_async_remote_copy(
            src_ref=stage[p].at[frm],
            dst_ref=recv[p].at[frm],
            send_sem=a2a_send.at[p, frm],
            recv_sem=a2a_recv.at[p, frm],
            device_id={"dp": frm},
            device_id_type=MESH,
        )

    for to_core in range(CORES):
        if to_core > 0:

            @pl.when(core == 1)
            def _():
                def gone(i, carry):
                    to = chip_peer(i, 0)

                    @pl.when(to != me)
                    def _():
                        for p in range(count):
                            unit_copy(p, to).wait_send()

                    return carry

                lax.fori_loop(0, GRID_X * GRID_Y, gone, 0)

        for p in range(count):
            if to_core == 0:
                for q, copy in loads:
                    if p == q:
                        copy.wait()
                recv[p][me] = held[p][inv_smem[0, me]]

            def send_unit(i, carry, p=p, to_core=to_core):
                to = chip_peer(i, to_core)

                @pl.when(to != me)
                def _():
                    stage[p][to] = held[p][inv_smem[0, to]]
                    pltpu.make_async_remote_copy(
                        src_ref=stage[p].at[to],
                        dst_ref=recv[p].at[me],
                        send_sem=a2a_send.at[p, to],
                        recv_sem=a2a_recv.at[p, me],
                        device_id={"dp": to},
                        device_id_type=MESH,
                    ).start()
                return carry

            lax.fori_loop(0, GRID_X * GRID_Y, send_unit, 0)
    for copy in weight_loads:
        copy.start()

    def table_arrived(o, carry):
        frm = peer(o)
        pltpu.make_async_remote_copy(
            src_ref=table_out,
            dst_ref=table_in.at[frm],
            send_sem=table_send.at[frm],
            recv_sem=table_recv.at[frm],
            device_id={"dp": frm},
            device_id_type=MESH,
        ).wait_recv()
        return carry

    lax.fori_loop(1, n_dp, table_arrived, 0)
    table = table_in[:, 0, :]
    wide = lax.broadcasted_iota(jnp.int32, (units, 128), 1)
    tall = lax.broadcasted_iota(jnp.int32, (units, 128), 0)
    place_col = jnp.sum(jnp.where(wide == me, table, 0), axis=1, keepdims=True)
    for n in range(units):
        place_smem[n] = jnp.max(jnp.where(tall == n, place_col, 0))
        source_smem[n] = jnp.max(jnp.where(place_col == n, tall, 0))

    block = DOC_UNITS * unit_rows
    score_scale = 1.0 / math.sqrt(HEAD)
    exponent_scale = score_scale * math.log2(math.e)

    def one_doc(p, doc):
        length = length_ref[doc]
        sources = [source_smem[doc * DOC_UNITS + i] for i in range(DOC_UNITS)]

        def rows(p, at):
            return jnp.concatenate(
                [recv[p][s, :, pl.ds(at, HEAD)] for s in sources], axis=0
            )

        key_at = lax.broadcasted_iota(jnp.int32, (block, block), 0)
        query_at = lax.broadcasted_iota(jnp.int32, (block, block), 1)
        allowed = (key_at <= query_at) & (key_at < length)
        live = lax.broadcasted_iota(jnp.int32, (block, HEAD), 0) < length
        keys, values = rows(0, 0), rows(0, kv_cols)
        if p == 0:
            key_grad = jnp.zeros((block, HEAD), jnp.float32)
            value_grad = jnp.zeros((block, HEAD), jnp.float32)
        else:
            key_grad, value_grad = kv_total[doc, 0], kv_total[doc, 1]

        def store(at, value):
            low = value.astype(jnp.bfloat16)
            for i in range(DOC_UNITS):
                grads[doc * DOC_UNITS + i, :, pl.ds(at, HEAD)] = low[
                    i * unit_rows : (i + 1) * unit_rows
                ]

        for n, head in enumerate(phases[p]):
            at = 2 * n * HEAD + (0 if p else 2 * kv_cols)
            queries = rows(p, at)
            masked = rows(p, at + HEAD)
            masked = jnp.where(live, masked, jnp.zeros_like(masked))
            scores = jnp.where(allowed, dot(keys, queries, NT), -1e30)
            peak = jnp.max(scores, axis=0, keepdims=True)
            expanded = jnp.exp2((scores - peak) * exponent_scale)
            probs = expanded * (1.0 / jnp.sum(expanded, axis=0, keepdims=True))
            probs_low = probs.astype(jnp.bfloat16)
            prob_grad = dot(values, masked, NT)
            delta = jnp.sum(probs_low.astype(jnp.float32) * prob_grad, axis=0, keepdims=True)
            score_low = (probs * (prob_grad - delta)).astype(jnp.bfloat16)
            value_grad += dot(probs_low, masked, NN)
            key_grad += dot(score_low, queries, NN)
            store(head * HEAD, dot(score_low, keys, TN) * score_scale)
        if p == count - 1:
            store(q_cols, key_grad * score_scale)
            store(q_cols + kv_cols, value_grad)
        else:
            kv_total[doc, 0] = key_grad
            kv_total[doc, 1] = value_grad

    for p in range(count):

        def unit_arrived(o, carry, p=p):
            unit_copy(p, peer(o)).wait_recv()
            return carry

        lax.fori_loop(1, n_dp, unit_arrived, 0)

        def doc_phase(doc, carry, p=p):
            one_doc(p, doc)
            return carry

        lax.fori_loop(0, docs, doc_phase, 0)
    for copy in weight_loads:
        copy.wait()

    chunks = units // CHUNK_UNITS
    chunk_rows = CHUNK_UNITS * unit_rows
    half = chunk_rows // 2
    out_cols = out_hbm.shape[2]
    far = n_mp // 2

    def part(chunk, distance):
        column = lax.rem(z + distance, n_mp) * out_cols
        return dot(
            lhs[chunk],
            weights[pl.ds(pl.multiple_of(column, out_cols), out_cols), :],
            NT,
        )

    def ring_copy(chunk, way, step):
        first, count = (0, chunk_rows) if step else (way * half, half)
        return pltpu.make_async_remote_copy(
            src_ref=ring_send.at[chunk, way, step, pl.ds(first, count), :],
            dst_ref=ring_recv.at[chunk, way, step, pl.ds(first, count), :],
            send_sem=ring_send_sem.at[chunk, way, step],
            recv_sem=ring_recv_sem.at[chunk, way, step],
            device_id={"mp": left if way else right},
            device_id_type=MESH,
        )

    def back_copy(o):
        to = peer(n_dp - 1 - o)
        return pltpu.make_async_remote_copy(
            src_ref=out_buf.at[o],
            dst_ref=out_hbm.at[me],
            send_sem=back_send.at[to],
            recv_sem=back_recv.at[me],
            device_id={"dp": to},
            device_id_type=MESH,
        )

    def first_step(chunk, carry):
        for i in range(CHUNK_UNITS):
            s = peer(n_dp - 1 - (chunk * CHUNK_UNITS + i))
            lhs[chunk, pl.ds(i * unit_rows, unit_rows), :] = grads[place_smem[s]]
        low = part(chunk, far).astype(jnp.bfloat16)
        for way in range(2):
            ring_send[chunk, way, 0, pl.ds(way * half, half), :] = low[
                way * half : (way + 1) * half
            ]
            ring_copy(chunk, way, 0).start()
        return carry

    lax.fori_loop(0, chunks, first_step, 0)

    for step in range(1, far):

        def next_step(chunk, carry, step=step):
            for way in range(2):
                total = part(chunk, n_mp - far + step if way else far - step)
                ring_copy(chunk, way, step - 1).wait_recv()
                for h in range(2):
                    piece = total[h * half : (h + 1) * half]
                    if step > 1 or h == way:
                        piece += ring_recv[
                            chunk, way, step - 1, pl.ds(h * half, half), :
                        ].astype(jnp.float32)
                    ring_send[chunk, way, step, pl.ds(h * half, half), :] = piece.astype(
                        jnp.bfloat16
                    )
                ring_copy(chunk, way, step).start()
            return carry

        lax.fori_loop(0, chunks, next_step, 0)

    own_copy = pltpu.make_async_copy(out_buf.at[n_dp - 1], out_hbm.at[me], small_sem.at[2])

    def last_step(chunk, carry):
        total = part(chunk, 0)
        for way in range(2):
            ring_copy(chunk, way, far - 1).wait_recv()
            total += ring_recv[chunk, way, far - 1].astype(jnp.float32)
        low = total.astype(jnp.bfloat16)
        for i in range(CHUNK_UNITS):
            out_buf[chunk * CHUNK_UNITS + i] = low[i * unit_rows : (i + 1) * unit_rows]
        for i in range(CHUNK_UNITS - 1):
            back_copy(chunk * CHUNK_UNITS + i).start()

        @pl.when(chunk < chunks - 1)
        def _():
            back_copy(chunk * CHUNK_UNITS + CHUNK_UNITS - 1).start()

        @pl.when(chunk == chunks - 1)
        def _():
            own_copy.start()

        return carry

    lax.fori_loop(0, chunks, last_step, 0)
    own_copy.wait()

    def exchange_done(o, carry):
        to = peer(o)
        pltpu.make_async_remote_copy(
            src_ref=table_out,
            dst_ref=table_in.at[to],
            send_sem=table_send.at[to],
            recv_sem=table_recv.at[to],
            device_id={"dp": to},
            device_id_type=MESH,
        ).wait_send()

        @pl.when((core == 0) | (lax.rem(to, CORES) == 1))
        def _():
            for p in range(count):
                unit_copy(p, to).wait_send()

        return carry

    lax.fori_loop(1, n_dp, exchange_done, 0)

    def ring_done(chunk, carry):
        for way in range(2):
            for step in range(far):
                ring_copy(chunk, way, step).wait_send()
        return carry

    lax.fori_loop(0, chunks, ring_done, 0)

    def back_arrived(o, carry):
        frm = peer(o)
        pltpu.make_async_remote_copy(
            src_ref=out_buf.at[o],
            dst_ref=out_hbm.at[frm],
            send_sem=back_send.at[frm],
            recv_sem=back_recv.at[frm],
            device_id={"dp": frm},
            device_id_type=MESH,
        ).wait()
        return carry

    lax.fori_loop(1, n_dp, back_arrived, 0)


def settle(server_hbm, back_hbm, out_hbm, server, held, wide, server_sem, in_sem, out_sem):
    units, unit_rows = held.shape[:2]
    rows = units * unit_rows // SETTLE_STEPS
    share = units // SETTLE_STEPS
    table = pltpu.make_async_copy(server_hbm, server, server_sem)

    def fetch(step):
        part = pl.ds(step * share, share)
        return pltpu.make_async_copy(back_hbm.at[part], held.at[part], in_sem.at[step])

    def emit(step):
        part = pl.ds(step * rows, rows)
        return pltpu.make_async_copy(wide.at[part, :], out_hbm.at[part, :], out_sem.at[step])

    table.start()
    for step in range(SETTLE_STEPS):
        fetch(step).start()
    table.wait()
    for step in range(SETTLE_STEPS):
        fetch(step).wait()
    for step in range(SETTLE_STEPS):
        for u in range(step * share, (step + 1) * share):
            wide[pl.ds(u * unit_rows, unit_rows), :] = held[server[u]].astype(jnp.float32)
        emit(step).start()
    for step in range(SETTLE_STEPS):
        emit(step).wait()


def local(
    saved_query,
    saved_key,
    saved_value,
    grad_output,
    unit_server,
    unit_place,
    doc_length,
    query_weight,
    key_weight,
    value_weight,
):
    n_dp, n_mp = lax.axis_size("dp"), lax.axis_size("mp")
    units = unit_server.shape[0]
    unit_rows = saved_query.shape[0] // units
    q_cols, kv_cols = saved_query.shape[1], saved_key.shape[1]
    out_all = query_weight.shape[0]
    out_cols = out_all // n_mp
    k_cols = q_cols + 2 * kv_cols
    heads = q_cols // HEAD
    phases = [range(h, h + 1) for h in range(heads)]
    widths = [2 * HEAD * len(p) for p in phases]
    widths[0] += 2 * kv_cols
    chunks = units // CHUNK_UNITS
    chunk_rows = CHUNK_UNITS * unit_rows
    far = n_mp // 2
    low = jnp.bfloat16

    def split(a):
        return a.reshape(units, unit_rows, a.shape[1])

    smem = pl.BlockSpec(memory_space=pltpu.SMEM)
    hbm = pl.BlockSpec(memory_space=pl.ANY)
    dma = pltpu.SemaphoreType.DMA
    back = pl.pallas_call(
        functools.partial(kernel, n_dp, n_mp, phases),
        out_shape=jax.ShapeDtypeStruct((n_dp, unit_rows, out_cols), low),
        in_specs=[smem] * 3 + [hbm] * 7,
        out_specs=hbm,
        scratch_shapes=[
            *[pltpu.VMEM((units, unit_rows, w), low) for w in widths],
            *[pltpu.VMEM((n_dp, unit_rows, w), low) for w in widths],
            *[pltpu.VMEM((n_dp, unit_rows, w), low) for w in widths],
            pltpu.VMEM((1, 128), jnp.int32),
            pltpu.VMEM((n_dp, 1, 128), jnp.int32),
            pltpu.VMEM((8, 128), jnp.int32),
            pltpu.SMEM((8, 128), jnp.int32),
            pltpu.SMEM((units,), jnp.int32),
            pltpu.SMEM((units,), jnp.int32),
            pltpu.VMEM((out_all, k_cols), low),
            pltpu.VMEM((units // DOC_UNITS, 2, DOC_UNITS * unit_rows, HEAD), jnp.float32),
            pltpu.VMEM((units, unit_rows, k_cols), low),
            pltpu.VMEM((chunks, chunk_rows, k_cols), low),
            pltpu.VMEM((chunks, 2, far, chunk_rows, out_cols), low),
            pltpu.VMEM((chunks, 2, far, chunk_rows, out_cols), low),
            pltpu.VMEM((units, unit_rows, out_cols), low),
            dma((2 + 2 * heads,)),
            dma((3,)),
            dma((3,)),
            dma((len(phases), n_dp)),
            dma((len(phases), n_dp)),
            dma((n_dp,)),
            dma((n_dp,)),
            dma((chunks, 2, far)),
            dma((chunks, 2, far)),
            dma((n_dp,)),
            dma((n_dp,)),
        ],
        compiler_params=pltpu.CompilerParams(
            collective_id=0, has_side_effects=True, vmem_limit_bytes=60 * 1024 * 1024
        ),
        name="attention_backward_exchange",
    )(
        unit_server,
        unit_place,
        doc_length,
        split(saved_query),
        split(saved_key),
        split(saved_value),
        split(grad_output),
        query_weight,
        key_weight,
        value_weight,
    )
    return pl.pallas_call(
        settle,
        out_shape=jax.ShapeDtypeStruct((units * unit_rows, out_cols), jnp.float32),
        in_specs=[hbm, hbm],
        out_specs=hbm,
        scratch_shapes=[
            pltpu.SMEM((units,), jnp.int32),
            pltpu.VMEM((units, unit_rows, out_cols), low),
            pltpu.VMEM((units * unit_rows, out_cols), jnp.float32),
            dma,
            dma((SETTLE_STEPS,)),
            dma((SETTLE_STEPS,)),
        ],
        name="settle_rows",
    )(unit_server, back)


def solution(mesh):
    placed = (
        P("dp", "mp"),
        P("dp", "mp"),
        P("dp", "mp"),
        P("dp", "mp"),
        P("dp"),
        P("dp"),
        P("dp"),
        P(None, "mp"),
        P(None, "mp"),
        P(None, "mp"),
    )
    return jax.shard_map(
        local, mesh=mesh, in_specs=placed, out_specs=P("dp", "mp"), check_vma=False
    )
```
